32 devices in a mesh: pipe: 4 (over y, x), ctx: 8 (over z, core).
Axes of the slice: x: 2, y: 2, z: 4, core: 2. Of those that a mesh axis runs over, the one named last changes fastest.
Arguments:
- queries: bfloat16 [4, 1024, 4096], P('pipe', 'ctx'), may hold values from -45 to 45
- keys_values: bfloat16 [4, 1024, 1024], P('pipe', 'ctx'), may hold values from -4 to 4
- out_grads: bfloat16 [4, 1024, 4096], P('pipe', 'ctx'), may hold values from -6 to 6
- doc_lengths: int32 [8], P('pipe'), may hold values from 1 to 384, 1024 in all
Outputs:
- query_grads: bfloat16 [4, 1024, 4096], P('pipe', 'ctx')
- key_value_grads: bfloat16 [4, 1024, 1024], P('pipe', 'ctx')
The draws below stay inside these ranges and needn't reach their ends.
Inputs may be any that keep to these rules, and one draw needn't show every extreme that they name: `doc_lengths`: the 8 lengths sum to 1024; the longest document has exactly 384 positions.
All inputs are finite; a program needn't handle non-finite values. No bound on the sum of `doc_lengths` on one device may be relied on, other than what follows from the above.
Results may differ from the reference program's by a relative error of at most 0.009.
Values may be sent and summed in bfloat16 or wider, within the bound.
No kernel may reach another device: no remote copies, remote signals or barrier semaphores. Data moves between devices by JAX's collectives and lax.ppermute only.
A program may use at most 64 MiB of HBM per device.

```python
import math
import jax
import jax.numpy as jnp
import numpy as np
from jax import lax

HQ = 32
HK = 4
HD = 128
TOK_DEV = 128
REACH = 3
SEQ = 1024
NDOC = 8
MAXDOC = 384
KEYS = 512
N_PIPE = 4
N_CTX = 8


def pair_arrays(key):
    query_key = jax.random.fold_in(key, 101)
    other_key = jax.random.fold_in(key, 202)
    query_width = HQ * HD
    pair_width = 2 * HK * HD
    queries = jnp.clip(jax.random.normal(query_key, (N_PIPE, SEQ, query_width), jnp.float32), -4.0, 4.0)
    keys_values = jnp.clip(jax.random.normal(other_key, (N_PIPE, SEQ, pair_width), jnp.float32), -4.0, 4.0)
    return (queries, keys_values)


def draw_queries(key, part):
    return pair_arrays(key)[0].astype(jnp.bfloat16)


def draw_keys_values(key, part):
    return pair_arrays(key)[1].astype(jnp.bfloat16)


def steps_of(stream_key, extent, shards, least, high):
    def one(dim, shards_of):
        steps = jax.random.uniform(jax.random.fold_in(jax.random.fold_in(stream_key, 6), dim), (shards_of,), jnp.float32, least / len(shards), high / len(shards))
        return jnp.repeat(jnp.exp(steps), extent[dim] // shards_of).reshape((-1,) + (1,) * (len(extent) - dim - 1))

    factor_of = one(*shards[0])
    for cut in shards[1:]:
        factor_of = factor_of * one(*cut)
    return factor_of


def profile(number_of, total, most, skew):
    weights = [(1 << 20) // math.isqrt(rank ** skew) + 1 for rank in range(2, number_of + 1)]
    spare, holding = total - most - (number_of - 1), [1] * (number_of - 1)
    while spare > 0:
        candidates = [i for i in range(number_of - 1) if holding[i] < most]
        pool, left = sum([weights[i] for i in candidates]), spare
        for i in candidates:
            addition = min(most - holding[i], max(1, left * weights[i] // pool), spare)
            holding[i] = holding[i] + addition
            spare = spare - addition
    return np.array([most] + holding)


def uneven_parts(own_key, count, total, reach, slope):
    if count == 2:
        one = jax.random.randint(own_key, (), max(1, total - reach), min(reach, total - 1) + 1)
        return jnp.stack([one, total - one])
    sizes = jnp.asarray(profile(count, total, reach, slope), jnp.int32)
    twos = (count - 1) // 2
    source_of, taker = sizes[1:1 + 2 * twos:2], sizes[2:2 + 2 * twos:2]
    slack = jnp.minimum(source_of - 1, reach - taker)
    shifted = jax.random.randint(jax.random.fold_in(own_key, 1), (twos,), 0, 1 << 20) % (slack + 1)
    sizes = sizes.at[1:1 + 2 * twos:2].set(source_of - shifted).at[2:2 + 2 * twos:2].set(taker + shifted)
    return sizes[jax.random.permutation(jax.random.fold_in(own_key, 2), count)]


def noise(own_key, shape, width, most, pieces=(), kind=jnp.bfloat16):
    factor_of = steps_of(own_key, shape, pieces, -0.22, 0.18) if pieces else 1.0
    array = jax.random.normal(own_key, shape, jnp.float32) * width * factor_of
    return jnp.minimum(jnp.maximum(array, -most), most).astype(kind)


def setup_inputs(seed: int = 0) -> dict:
    key_list = jax.random.split(jax.random.key(seed), 5)
    return {
        "queries": draw_queries(jax.random.fold_in(key_list[4], 71), 0),
        "keys_values": draw_keys_values(jax.random.fold_in(key_list[4], 71), 0),
        "out_grads": noise(key_list[2], (N_PIPE, SEQ, HQ * HD), 1.0, 6.0, ((0, 4), (1, 8))),
        "doc_lengths": uneven_parts(key_list[3], NDOC, SEQ, MAXDOC, 2).astype(jnp.int32),
    }


def doc_of(starts, position):
    return lax.optimization_barrier(jnp.sum((starts[None, :] <= position[:, None]).astype(jnp.int32), axis=1)) - 1

def attend(q_block, kv_window, dout_block, allowed):
    q_rows = q_block.shape[0]
    key_rows = kv_window.shape[0]
    group_size = HQ // HK
    score_scale = 1.0 / math.sqrt(HD)
    highest = lax.Precision.HIGHEST

    def per_group(head_group):
        q_part = lax.dynamic_slice_in_dim(q_block, head_group * group_size * HD, group_size * HD, 1)
        q_part = q_part.reshape(q_rows, group_size, HD).astype(jnp.float32)
        d_part = lax.dynamic_slice_in_dim(dout_block, head_group * group_size * HD, group_size * HD, 1)
        d_part = d_part.reshape(q_rows, group_size, HD).astype(jnp.float32)
        k_part = lax.dynamic_slice_in_dim(kv_window, head_group * HD, HD, 1).astype(jnp.float32)
        v_part = lax.dynamic_slice_in_dim(kv_window, HK * HD + head_group * HD, HD, 1).astype(jnp.float32)
        scores = jnp.einsum('tgd,kd->gtk', q_part, k_part, precision=highest) * score_scale
        scores = jnp.where(allowed[None], scores, -1e+30)
        biggest = lax.optimization_barrier(jnp.max(scores, axis=-1, keepdims=True))
        expo = jnp.where(allowed[None], jnp.exp(scores - biggest), 0.0)
        weights = expo / lax.optimization_barrier(jnp.sum(expo, axis=-1, keepdims=True))
        weights_low = weights.astype(jnp.bfloat16).astype(jnp.float32)
        attended = jnp.einsum('gtk,kd->tgd', weights_low, v_part, precision=highest)
        delta = lax.optimization_barrier(jnp.sum(d_part * attended, axis=-1))
        dweights = jnp.einsum('tgd,kd->gtk', d_part, v_part, precision=highest)
        dscores = (weights * (dweights - jnp.transpose(delta)[:, :, None])).astype(jnp.bfloat16).astype(jnp.float32)
        q_grad = jnp.einsum('gtk,kd->tgd', dscores, k_part, precision=highest) * score_scale
        k_grad = jnp.einsum('gtk,tgd->kd', dscores, q_part, precision=highest) * score_scale
        v_grad = jnp.einsum('gtk,tgd->kd', weights_low, d_part, precision=highest)
        return (q_grad.reshape(q_rows, group_size * HD).astype(jnp.bfloat16), k_grad, v_grad)
    q_grads, k_grads, v_grads = lax.map(per_group, jnp.arange(HK, dtype=jnp.int32))
    q_grads = jnp.moveaxis(q_grads, 0, 1).reshape(q_rows, HQ * HD)
    k_grads = jnp.moveaxis(k_grads, 0, 1).reshape(key_rows, HK * HD)
    v_grads = jnp.moveaxis(v_grads, 0, 1).reshape(key_rows, HK * HD)
    return (q_grads, jnp.concatenate([k_grads, v_grads], axis=1))

def reference(queries, keys_values, out_grads, doc_lengths):
    starts = (jnp.cumsum(doc_lengths) - doc_lengths).astype(jnp.int32)
    shard_rows = TOK_DEV
    padding = REACH * shard_rows
    window_rows = KEYS

    def section(operands):
        q_all, kv_all, dout_all = operands
        kv_padded = jnp.concatenate([jnp.zeros((padding, kv_all.shape[1]), kv_all.dtype), kv_all], axis=0)

        def block(accum, block_index):
            first = (block_index * shard_rows).astype(jnp.int32)
            q_block = lax.dynamic_slice_in_dim(q_all, first, shard_rows, 0)
            d_block = lax.dynamic_slice_in_dim(dout_all, first, shard_rows, 0)
            kv_window = lax.dynamic_slice_in_dim(kv_padded, first, window_rows, 0)
            q_position = first + jnp.arange(shard_rows, dtype=jnp.int32)
            k_position = first - padding + jnp.arange(window_rows, dtype=jnp.int32)
            allowed = (doc_of(starts, q_position)[:, None] == doc_of(starts, k_position)[None, :]) & (k_position[None, :] <= q_position[:, None])
            q_grads, kv_grads = attend(q_block, kv_window, d_block, allowed)
            current = lax.dynamic_slice_in_dim(accum, first, window_rows, 0)
            accum = lax.dynamic_update_slice_in_dim(accum, current + kv_grads, first, 0)
            return (accum, q_grads)
        accum = jnp.zeros((padding + SEQ, kv_all.shape[1]), jnp.float32)
        accum, q_grads = lax.scan(block, accum, jnp.arange(N_CTX, dtype=jnp.int32))
        return (q_grads.reshape(SEQ, HQ * HD), accum[padding:].astype(jnp.bfloat16))
    query_grads, key_value_grads = lax.map(section, (queries, keys_values, out_grads))
    return (query_grads, key_value_grads)
```

```python
import functools
import math

import jax
import jax.numpy as jnp
from jax import lax
from jax.experimental import pallas as pl
from jax.experimental.pallas import tpu as pltpu
from jax.sharding import PartitionSpec as P

HQ = 32
HK = 4
HD = 128
REACH = 3
GROUP = HQ // HK
F32 = jnp.float32
BF16 = jnp.bfloat16
NT = (((1,), (1,)), ((), ()))
NN = (((1,), (0,)), ((), ()))


def moved(value, target_of):
    count = lax.axis_size("ctx")
    pairs = [(i, target_of(i)) for i in range(count)]
    return lax.ppermute(value, "ctx", [(s, t) for s, t in pairs if 0 <= t < count])


def one_three(value):
    return moved(value, lambda i: i + 1 if i % 2 else i + 3)


def one_three_back(value):
    return moved(value, lambda i: i - 3 if i % 2 else i - 1)


def three_one(value):
    return moved(value, lambda i: i + 3 if i % 2 else i + 1)


def three_one_back(value):
    return moved(value, lambda i: i - 1 if i % 2 else i - 3)


def swapped(value):
    return moved(value, lambda i: i ^ 1)


def all_lengths_by_xor(lengths):
    count = lax.axis_size("pipe")
    stride = 1
    while stride < count:
        other = lax.ppermute(lengths, "pipe", [(i, i ^ stride) for i in range(count)])
        lengths = jnp.concatenate([lengths, other])
        stride *= 2
    return lengths


def kernel(per_pipe, lens_ref, q_ref, d_ref, kv0_ref, kv1_ref, kv2_ref, kv3_ref,
           dq_ref, g0_ref, g1_ref, g2_ref, g3_ref,
           bias_scr, kt_scr, s_scr, p_scr, dp_scr, ds_scr, w_scr):
    rows = q_ref.shape[0]
    blocks = REACH + 1
    g = pl.program_id(0)
    here = lax.axis_index("ctx")
    pipe = lax.axis_index("pipe")
    odd = lax.rem(here, 2)
    offsets = (0, 1 + 2 * odd, 2, 3 - 2 * odd)
    kv_refs = (kv0_ref, kv1_ref, kv2_ref, kv3_ref)
    g_refs = (g0_ref, g1_ref, g2_ref, g3_ref)

    @pl.when(g == 0)
    def _():
        t_pos = here * rows + lax.broadcasted_iota(jnp.int32, (1, rows), 1)
        total = lens_ref.shape[0]

        def step(d, carry):
            start, doc_start = carry
            slot = ((d // per_pipe) ^ pipe) * per_pipe + d % per_pipe
            doc_start = jnp.where(t_pos >= start, start, doc_start)
            return start + lens_ref[slot], doc_start

        _, doc_start = lax.fori_loop(
            0, total, step, (jnp.int32(0), jnp.zeros((1, rows), jnp.int32))
        )
        for b in range(blocks):
            u_pos = (here - offsets[b]) * rows + lax.broadcasted_iota(jnp.int32, (rows, rows), 0)
            ok = (u_pos >= doc_start) & (u_pos <= t_pos)
            bias_scr[b] = jnp.where(ok, 0.0, -1e30).astype(F32)

    kcol = pl.ds(pl.multiple_of(g * HD, HD), HD)
    vcol = pl.ds(pl.multiple_of(HK * HD + g * HD, HD), HD)
    for b in range(blocks):
        kt_scr[:, b * rows:(b + 1) * rows] = kv_refs[b][:, kcol].T
    scale = 1.0 / math.sqrt(HD)
    c = scale * math.log2(math.e)
    for pair in range(GROUP // 2):
        lo, hi = 2 * pair * HD, (2 * pair + 1) * HD
        q2 = jnp.concatenate([q_ref[:, lo:lo + HD], q_ref[:, hi:hi + HD]], axis=0)
        d2 = jnp.concatenate([d_ref[:, lo:lo + HD], d_ref[:, hi:hi + HD]], axis=0)
        biggest = None
        for b in range(blocks):
            s = lax.dot_general(kv_refs[b][:, kcol], q2, NT, preferred_element_type=F32)
            s = s + jnp.concatenate([bias_scr[b]] * 2, axis=1)
            s_scr[b] = s
            top = jnp.max(s, axis=0, keepdims=True)
            biggest = top if biggest is None else jnp.maximum(biggest, top)
        total = dot = None
        for b in range(blocks):
            p = jnp.exp2((s_scr[b] - biggest) * c)
            dp = lax.dot_general(kv_refs[b][:, vcol], d2, NT, preferred_element_type=F32)
            p_scr[b] = p
            dp_scr[b] = dp
            sp = jnp.sum(p, axis=0, keepdims=True)
            sd = jnp.sum(p * dp, axis=0, keepdims=True)
            total = sp if total is None else total + sp
            dot = sd if dot is None else dot + sd
        inv = 1.0 / total
        delta = dot * inv
        columns = slice(2 * pair * rows, 2 * (pair + 1) * rows)
        for b in range(blocks):
            w = p_scr[b] * inv
            ds_scr[b * rows:(b + 1) * rows, columns] = (w * (dp_scr[b] - delta)).astype(BF16)
            w_scr[b * rows:(b + 1) * rows, columns] = w.astype(BF16)
        dqt = lax.dot_general(kt_scr[...], ds_scr[:, columns], NN, preferred_element_type=F32)
        dq = (dqt * scale).astype(BF16).T
        dq_ref[:, lo:lo + HD] = dq[:rows]
        dq_ref[:, hi:hi + HD] = dq[rows:]
    qs = jnp.concatenate([q_ref[:, h * HD:(h + 1) * HD] for h in range(GROUP)], axis=0)
    dk = lax.dot_general(ds_scr[...], qs, NN, preferred_element_type=F32) * scale
    dos = jnp.concatenate([d_ref[:, h * HD:(h + 1) * HD] for h in range(GROUP)], axis=0)
    dv = lax.dot_general(w_scr[...], dos, NN, preferred_element_type=F32)
    for b in range(blocks):
        part = slice(b * rows, (b + 1) * rows)
        g_refs[b][:, kcol] = dk[part].astype(g_refs[b].dtype)
        g_refs[b][:, vcol] = dv[part].astype(g_refs[b].dtype)


def attention(per_pipe, lens, q, dout, kv0, kv1, kv2, kv3):
    rows = q.shape[0]
    wide = kv0.shape[1]
    keys = (REACH + 1) * rows
    head = pl.BlockSpec((rows, GROUP * HD), lambda g: (0, g))
    whole = pl.BlockSpec((rows, wide), lambda g: (0, 0))
    like = lambda dtype: jax.ShapeDtypeStruct((rows, wide), dtype)
    return pl.pallas_call(
        functools.partial(kernel, per_pipe),
        grid=(HK,),
        in_specs=[pl.BlockSpec(memory_space=pltpu.SMEM), head, head, whole, whole, whole, whole],
        out_specs=[head, whole, whole, whole, whole],
        out_shape=[jax.ShapeDtypeStruct(q.shape, BF16), like(F32), like(BF16), like(BF16), like(BF16)],
        scratch_shapes=[
            pltpu.VMEM((REACH + 1, rows, rows), F32),
            pltpu.VMEM((HD, keys), BF16),
            pltpu.VMEM((REACH + 1, rows, 2 * rows), F32),
            pltpu.VMEM((REACH + 1, rows, 2 * rows), F32),
            pltpu.VMEM((REACH + 1, rows, 2 * rows), F32),
            pltpu.VMEM((keys, GROUP * rows), BF16),
            pltpu.VMEM((keys, GROUP * rows), BF16),
        ],
        name="attention",
    )(lens, q, dout, kv0, kv1, kv2, kv3)


def on_device(queries, keys_values, out_grads, doc_lengths):
    kv = keys_values[0]
    near = one_three(kv)
    far = three_one(kv)
    lens = all_lengths_by_xor(doc_lengths)
    side = swapped(near)
    dq, own, g_near, g_side, g_far = attention(
        doc_lengths.shape[0], lens, queries[0], out_grads[0], kv, near, side, far
    )
    back = three_one_back(g_far)
    joined = (g_near.astype(F32) + swapped(g_side).astype(F32)).astype(BF16)
    total = own + back.astype(F32) + one_three_back(joined).astype(F32)
    return (dq[None], total.astype(BF16)[None])


def solution(mesh):
    spec = P("pipe", "ctx", None)
    return jax.shard_map(
        on_device,
        mesh=mesh,
        in_specs=(spec, spec, spec, P("pipe")),
        out_specs=(spec, spec),
        check_vma=False,
    )
```

```python
import functools
import math

import jax
import jax.numpy as jnp
from jax import lax
from jax.experimental import pallas as pl
from jax.experimental.pallas import tpu as pltpu
from jax.sharding import PartitionSpec as P


HQ = 32
HK = 4
HD = 128
REACH = 3
GROUP = HQ // HK
F32 = jnp.float32
BF16 = jnp.bfloat16
NT = (((1,), (1,)), ((), ()))
NN = (((1,), (0,)), ((), ()))
SCALE = 1.0 / math.sqrt(HD)
RATE = SCALE * math.log2(math.e)
PAIRS = HQ // 2


def moved(value, target_of):
    count = lax.axis_size("ctx")
    pairs = [(i, target_of(i)) for i in range(count)]
    return lax.ppermute(value, "ctx", [(s, t) for s, t in pairs if 0 <= t < count])


def one_three(value):
    return moved(value, lambda i: i + 1 if i % 2 else i + 3)


def one_three_back(value):
    return moved(value, lambda i: i - 3 if i % 2 else i - 1)


def three_one(value):
    return moved(value, lambda i: i + 3 if i % 2 else i + 1)


def three_one_back(value):
    return moved(value, lambda i: i - 1 if i % 2 else i - 3)


def swapped(value):
    return moved(value, lambda i: i ^ 1)


def all_lengths_by_xor(lengths):
    count = lax.axis_size("pipe")
    stride = 1
    while stride < count:
        other = lax.ppermute(lengths, "pipe", [(i, i ^ stride) for i in range(count)])
        lengths = jnp.concatenate([lengths, other])
        stride *= 2
    return lengths


def fill_bias(per_pipe, lens_ref, bias_scr, offsets, rows):
    here = lax.axis_index("ctx")
    pipe = lax.axis_index("pipe")
    t_pos = here * rows + lax.broadcasted_iota(jnp.int32, (1, rows), 1)

    def step(d, carry):
        start, doc_start = carry
        slot = ((d // per_pipe) ^ pipe) * per_pipe + d % per_pipe
        doc_start = jnp.where(t_pos >= start, start, doc_start)
        return start + lens_ref[slot], doc_start

    _, doc_start = lax.fori_loop(
        0, lens_ref.shape[0], step, (jnp.int32(0), jnp.zeros((1, rows), jnp.int32))
    )
    for b, offset in enumerate(offsets):
        u_pos = (here - offset) * rows + lax.broadcasted_iota(jnp.int32, (rows, rows), 0)
        ok = (u_pos >= doc_start) & (u_pos <= t_pos)
        bias_scr[b * rows:(b + 1) * rows] = jnp.where(ok, 0.0, -1e30).astype(F32)


def offsets_of_moved():
    odd = lax.rem(lax.axis_index("ctx"), 2)
    return (1 + 2 * odd, 2, 3 - 2 * odd)


def at(i, width):
    return pl.ds(pl.multiple_of(i * width, width), width)


def stacked(ref, i):
    return jnp.concatenate([ref[:, at(2 * i, HD)], ref[:, at(2 * i + 1, HD)]], axis=0)


def tall(refs, column):
    return jnp.concatenate([ref[:, at(column, HD)] for ref in refs], axis=0)


def keys_of(refs, i):
    return tall(refs, i // (GROUP // 2))


def values_of(refs, i):
    return tall(refs, HK + i // (GROUP // 2))


def scores_of(refs, q_ref, bias_scr, i):
    s = lax.dot_general(keys_of(refs, i), stacked(q_ref, i), NT, preferred_element_type=F32)
    bias = bias_scr[...]
    return s + jnp.concatenate([bias, bias], axis=1)


def dweights_of(refs, d_ref, i):
    return lax.dot_general(values_of(refs, i), stacked(d_ref, i), NT, preferred_element_type=F32)


def pipelined(stages, count):
    depth = len(stages)
    for i in range(depth - 1):
        for k in range(i + 1):
            stages[k](i - k)

    def body(i, _):
        for k in range(depth):
            stages[k](i - k)
        return 0

    lax.fori_loop(depth - 1, count, body, 0)
    for i in range(count, count + depth - 1):
        for k in range(i - count + 1, depth):
            stages[k](i - k)


def own_stats_kernel(per_pipe, lens_ref, q_ref, d_ref, kv_ref, stats_ref, bias_scr, s_scr, dp_scr):
    rows = q_ref.shape[0]
    fill_bias(per_pipe, lens_ref, bias_scr, (0,), rows)

    def first(i):
        s_scr[i % 2] = scores_of([kv_ref], q_ref, bias_scr, i)
        dp_scr[i % 2] = dweights_of([kv_ref], d_ref, i)

    def second(i):
        s = s_scr[i % 2]
        top = jnp.max(s, axis=0, keepdims=True)
        p = jnp.exp2((s - top) * RATE)
        column = at(i, 2 * rows)
        stats_ref[0:1, column] = top
        stats_ref[1:2, column] = jnp.sum(p, axis=0, keepdims=True)
        stats_ref[2:3, column] = jnp.sum(p * dp_scr[i % 2], axis=0, keepdims=True)

    pipelined([first, second], PAIRS)


def moved_kernel(per_pipe, lens_ref, q_ref, d_ref, kv1_ref, kv2_ref, kv3_ref, stats_ref,
                 final_ref, g1_ref, g2_ref, g3_ref,
                 bias_scr, s_scr, dp_scr, p_scr, top_scr, acc_scr):
    rows = q_ref.shape[0]
    refs = [kv1_ref, kv2_ref, kv3_ref]
    fill_bias(per_pipe, lens_ref, bias_scr, offsets_of_moved(), rows)
    acc_scr[...] = jnp.zeros_like(acc_scr)

    def first(i):
        s = scores_of(refs, q_ref, bias_scr, i)
        s_scr[i % 2] = s
        own = stats_ref[0:1, at(i, 2 * rows)]
        top_scr[pl.ds(i % 2, 1)] = jnp.maximum(own, jnp.max(s, axis=0, keepdims=True))
        dp_scr[i % 3] = dweights_of(refs, d_ref, i)

    def second(i):
        column = at(i, 2 * rows)
        top = top_scr[pl.ds(i % 2, 1)]
        p = jnp.exp2((s_scr[i % 2] - top) * RATE)
        p_scr[i % 2] = p
        own = jnp.exp2((stats_ref[0:1, column] - top) * RATE)
        total = stats_ref[1:2, column] * own + jnp.sum(p, axis=0, keepdims=True)
        dot = stats_ref[2:3, column] * own + jnp.sum(p * dp_scr[i % 3], axis=0, keepdims=True)
        inv = 1.0 / total
        final_ref[0:1, column] = top
        final_ref[1:2, column] = inv
        final_ref[2:3, column] = dot * inv

    def third(i):
        column = at(i, 2 * rows)
        w = p_scr[i % 2] * final_ref[1:2, column]
        ds = (w * (dp_scr[i % 3] - final_ref[2:3, column])).astype(BF16)
        group = i // (GROUP // 2)
        acc_scr[:, at(group, HD)] += lax.dot_general(
            ds, stacked(q_ref, i), NN, preferred_element_type=F32
        )
        acc_scr[:, at(HK + group, HD)] += lax.dot_general(
            w.astype(BF16), stacked(d_ref, i), NN, preferred_element_type=F32
        )

    pipelined([first, second, third], PAIRS)
    for b, g_ref in enumerate((g1_ref, g2_ref, g3_ref)):
        part = slice(b * rows, (b + 1) * rows)
        g_ref[:, :HK * HD] = (acc_scr[part, :HK * HD] * SCALE).astype(BF16)
        g_ref[:, HK * HD:] = acc_scr[part, HK * HD:].astype(BF16)


def query_kernel(per_pipe, lens_ref, q_ref, d_ref, kv0_ref, kv1_ref, kv2_ref, kv3_ref, final_ref,
                 dq_ref, own_ref, bias_scr, kt_scr, s_scr, dp_scr, ds_scr, w_scr):
    rows = q_ref.shape[0]
    refs = [kv0_ref, kv1_ref, kv2_ref, kv3_ref]
    fill_bias(per_pipe, lens_ref, bias_scr, (0,) + offsets_of_moved(), rows)
    own_ref[...] = jnp.zeros_like(own_ref)
    for group in range(HK):
        for b, ref in enumerate(refs):
            kt_scr[group, :, b * rows:(b + 1) * rows] = ref[:, group * HD:(group + 1) * HD].T

    def first(i):
        s_scr[i % 2] = scores_of(refs, q_ref, bias_scr, i)
        dp_scr[i % 2] = dweights_of(refs, d_ref, i)

    def second(i):
        column = at(i, 2 * rows)
        p = jnp.exp2((s_scr[i % 2] - final_ref[0:1, column]) * RATE)
        w = p * final_ref[1:2, column]
        ds_scr[i % 2] = (w * (dp_scr[i % 2] - final_ref[2:3, column])).astype(BF16)
        w_scr[i % 2] = w[:rows].astype(BF16)

    def third(i):
        group = i // (GROUP // 2)
        own_ref[:, at(group, HD)] += SCALE * lax.dot_general(
            ds_scr[i % 2, :rows], stacked(q_ref, i), NN, preferred_element_type=F32
        )
        own_ref[:, at(HK + group, HD)] += lax.dot_general(
            w_scr[i % 2], stacked(d_ref, i), NN, preferred_element_type=F32
        )
        dqt = lax.dot_general(kt_scr[group], ds_scr[i % 2], NN, preferred_element_type=F32)
        dq = (dqt * SCALE).astype(BF16).T
        dq_ref[:, at(2 * i, HD)] = dq[:rows]
        dq_ref[:, at(2 * i + 1, HD)] = dq[rows:]

    pipelined([first, second, third], PAIRS)


def call(body, per_pipe, args, outs, scratch, matmul_rows):
    specs = [pl.BlockSpec(memory_space=pltpu.SMEM)]
    specs += [pl.BlockSpec(memory_space=pltpu.VMEM)] * (len(args) - 1)
    return pl.pallas_call(
        functools.partial(body, per_pipe),
        in_specs=specs,
        out_specs=[pl.BlockSpec(memory_space=pltpu.VMEM)] * len(outs),
        out_shape=outs,
        scratch_shapes=scratch,
        cost_estimate=pl.CostEstimate(
            flops=2 * HQ * HD * HD * matmul_rows,
            bytes_accessed=sum(x.size * x.dtype.itemsize for x in list(args) + list(outs)),
            transcendentals=0,
        ),
    )(*args)


def on_device(queries, keys_values, out_grads, doc_lengths):
    kv, q, dout = keys_values[0], queries[0], out_grads[0]
    rows, wide = kv.shape
    per_pipe = doc_lengths.shape[0]
    array = jax.ShapeDtypeStruct
    stat = array((8, HQ * rows), F32)
    blocks = REACH * rows
    keys = blocks + rows
    near = one_three(kv)
    far = three_one(kv)
    lens = all_lengths_by_xor(doc_lengths)
    (stats,) = call(
        own_stats_kernel, per_pipe, (lens, q, dout, kv), [stat],
        [pltpu.VMEM((rows, rows), F32)] + [pltpu.VMEM((2, rows, 2 * rows), F32)] * 2,
        2 * rows,
    )
    side = swapped(near)
    final, g_near, g_side, g_far = call(
        moved_kernel, per_pipe, (lens, q, dout, near, side, far, stats),
        [stat] + [array((rows, wide), BF16)] * 3,
        [
            pltpu.VMEM((blocks, rows), F32),
            pltpu.VMEM((2, blocks, 2 * rows), F32),
            pltpu.VMEM((3, blocks, 2 * rows), F32),
            pltpu.VMEM((2, blocks, 2 * rows), F32),
            pltpu.VMEM((2, 2 * rows), F32),
            pltpu.VMEM((blocks, wide), F32),
        ],
        4 * blocks,
    )
    back = three_one_back(g_far)
    side_back = swapped(g_side)
    joined = (g_near.astype(F32) + side_back.astype(F32)).astype(BF16)
    near_back = one_three_back(joined)
    dq, own = call(
        query_kernel, per_pipe, (lens, q, dout, kv, near, side, far, final),
        [array(q.shape, BF16), array((rows, wide), F32)],
        [
            pltpu.VMEM((keys, rows), F32),
            pltpu.VMEM((HK, HD, keys), BF16),
            pltpu.VMEM((2, keys, 2 * rows), F32),
            pltpu.VMEM((2, keys, 2 * rows), F32),
            pltpu.VMEM((2, keys, 2 * rows), BF16),
            pltpu.VMEM((2, rows, 2 * rows), BF16),
        ],
        4 * keys,
    )
    total = own + back.astype(F32) + near_back.astype(F32)
    return (dq[None], total.astype(BF16)[None])


def solution(mesh):
    spec = P("pipe", "ctx", None)
    return jax.shard_map(
        on_device,
        mesh=mesh,
        in_specs=(spec, spec, spec, P("pipe")),
        out_specs=(spec, spec),
        check_vma=False,
    )
```

```python
import functools
import math

import jax
import jax.numpy as jnp
from jax import lax
from jax.experimental import pallas as pl
from jax.experimental.pallas import tpu as pltpu
from jax.sharding import PartitionSpec as P


HQ = 32
HK = 4
HD = 128
REACH = 3
GROUP = HQ // HK
F32 = jnp.float32
BF16 = jnp.bfloat16
NT = (((1,), (1,)), ((), ()))
NN = (((1,), (0,)), ((), ()))
SCALE = 1.0 / math.sqrt(HD)
PAIRS = HQ // 2
SLOTS = GROUP // 2


def moved(value, target_of):
    count = lax.axis_size("ctx")
    pairs = [(i, target_of(i)) for i in range(count)]
    return lax.ppermute(value, "ctx", [(s, t) for s, t in pairs if 0 <= t < count])


def one_three(value):
    return moved(value, lambda i: i + 1 if i % 2 else i + 3)


def one_three_back(value):
    return moved(value, lambda i: i - 3 if i % 2 else i - 1)


def three_one(value):
    return moved(value, lambda i: i + 3 if i % 2 else i + 1)


def three_one_back(value):
    return moved(value, lambda i: i - 1 if i % 2 else i - 3)


def swapped(value):
    return moved(value, lambda i: i ^ 1)


def all_lengths(lengths):
    count = lax.axis_size("pipe")
    pieces, stride = [lengths], 1
    while stride < count:
        pieces.append(
            lax.ppermute(jnp.concatenate(pieces), "pipe", [(i, i ^ stride) for i in range(count)])
        )
        stride *= 2
    return pieces


def fill_bias(lens_refs, starts_scr, bias_scr, offsets, rows):
    here = lax.axis_index("ctx")
    pipe = lax.axis_index("pipe")
    t_pos = here * rows + lax.broadcasted_iota(jnp.int32, (1, rows), 1)
    per_pipe = lens_refs[0].shape[0]
    place = 0
    for ref in lens_refs:
        for k in range(ref.shape[0]):
            starts_scr[((place // per_pipe) ^ pipe) * per_pipe + place % per_pipe] = ref[k]
            place += 1

    def step(d, carry):
        start, doc_start = carry
        doc_start = jnp.where(t_pos >= start, start, doc_start)
        return start + starts_scr[d], doc_start

    _, doc_start = lax.fori_loop(0, place, step, (jnp.int32(0), jnp.zeros((1, rows), jnp.int32)))
    for b, offset in enumerate(offsets):
        u_pos = (here - offset) * rows + lax.broadcasted_iota(jnp.int32, (rows, rows), 0)
        ok = (u_pos >= doc_start) & (u_pos <= t_pos)
        bias_scr[b * rows:(b + 1) * rows] = jnp.where(ok, 0.0, -1e30).astype(F32)


def offsets_of_moved():
    odd = lax.rem(lax.axis_index("ctx"), 2)
    return (1 + 2 * odd, 2, 3 - 2 * odd)


def at(i, width):
    return pl.ds(pl.multiple_of(i * width, width), width)


def stacked(ref, i):
    return jnp.concatenate([ref[:, at(2 * i, HD)], ref[:, at(2 * i + 1, HD)]], axis=0)


def tall(refs, column):
    return jnp.concatenate([ref[:, at(column, HD)] for ref in refs], axis=0)


def keys_of(refs, i):
    return tall(refs, i // (GROUP // 2))


def values_of(refs, i):
    return tall(refs, HK + i // (GROUP // 2))


def scores_of(refs, q_ref, bias_scr, i):
    s = lax.dot_general(keys_of(refs, i), stacked(q_ref, i), NT, preferred_element_type=F32)
    bias = bias_scr[...]
    return s + jnp.concatenate([bias, bias], axis=1)


def dweights_of(refs, d_ref, i):
    return lax.dot_general(values_of(refs, i), stacked(d_ref, i), NT, preferred_element_type=F32)


def pipelined(stages):
    depth = len(stages)

    def steps(base, count, first, last):
        for j in range(count):
            for k in range(depth):
                if first <= j - k < last:
                    stages[k](base + (j - k), (j - k) % SLOTS)

    steps(0, SLOTS, 0, SLOTS)

    def body(trip, _):
        steps(trip * SLOTS, SLOTS, -SLOTS, SLOTS)
        return 0

    lax.fori_loop(1, PAIRS // SLOTS, body, 0)
    steps(PAIRS, depth - 1, -SLOTS, 0)


def own_stats_kernel(n_lens, *refs):
    lens_refs, refs = refs[:n_lens], refs[n_lens:]
    q_ref, d_ref, kv_ref, stats_ref, starts_scr, bias_scr, s_scr, dp_scr = refs
    rows = q_ref.shape[0]
    fill_bias(lens_refs, starts_scr, bias_scr, (0,), rows)

    def first(i, slot):
        s_scr[slot] = scores_of([kv_ref], q_ref, bias_scr, i)
        dp_scr[slot] = dweights_of([kv_ref], d_ref, i)

    def second(i, slot):
        s = s_scr[slot]
        top = jnp.max(s, axis=0, keepdims=True)
        p = jnp.exp((s - top) * SCALE)
        column = at(i, 2 * rows)
        stats_ref[0:1, column] = top
        stats_ref[1:2, column] = jnp.sum(p, axis=0, keepdims=True)
        stats_ref[2:3, column] = jnp.sum(p * dp_scr[slot], axis=0, keepdims=True)

    pipelined([first, second])


def moved_kernel(n_lens, *refs):
    lens_refs, refs = refs[:n_lens], refs[n_lens:]
    q_ref, d_ref, kv1_ref, kv2_ref, kv3_ref, stats_ref = refs[:6]
    final_ref, g1_ref, g2_ref, g3_ref = refs[6:10]
    starts_scr, bias_scr, s_scr, dp_scr, p_scr, row_scr, acc_scr = refs[10:]
    rows = q_ref.shape[0]
    refs = [kv1_ref, kv2_ref, kv3_ref]
    fill_bias(lens_refs, starts_scr, bias_scr, offsets_of_moved(), rows)
    acc_scr[...] = jnp.zeros_like(acc_scr)

    def first(i, slot):
        s = scores_of(refs, q_ref, bias_scr, i)
        s_scr[slot] = s
        own = stats_ref[0:1, at(i, 2 * rows)]
        row_scr[slot, 0:1] = jnp.maximum(own, jnp.max(s, axis=0, keepdims=True))
        dp_scr[slot] = dweights_of(refs, d_ref, i)

    def second(i, slot):
        column = at(i, 2 * rows)
        top = row_scr[slot, 0:1]
        p = jnp.exp((s_scr[slot] - top) * SCALE)
        p_scr[slot] = p
        own = jnp.exp((stats_ref[0:1, column] - top) * SCALE)
        total = stats_ref[1:2, column] * own + jnp.sum(p, axis=0, keepdims=True)
        dot = stats_ref[2:3, column] * own + jnp.sum(p * dp_scr[slot], axis=0, keepdims=True)
        inv = 1.0 / total
        delta = dot * inv
        row_scr[slot, 1:2] = inv
        row_scr[slot, 2:3] = delta
        final_ref[0:1, column] = top
        final_ref[1:2, column] = inv
        final_ref[2:3, column] = delta

    def third(i, slot):
        w = p_scr[slot] * row_scr[slot, 1:2]
        ds = (w * (dp_scr[slot] - row_scr[slot, 2:3])).astype(BF16)
        group = i // SLOTS
        acc_scr[:, at(group, HD)] += lax.dot_general(
            ds, stacked(q_ref, i), NN, preferred_element_type=F32
        )
        acc_scr[:, at(HK + group, HD)] += lax.dot_general(
            w.astype(BF16), stacked(d_ref, i), NN, preferred_element_type=F32
        )

    pipelined([first, second, third])
    for b, g_ref in enumerate((g1_ref, g2_ref, g3_ref)):
        part = slice(b * rows, (b + 1) * rows)
        g_ref[:, :HK * HD] = (acc_scr[part, :HK * HD] * SCALE).astype(BF16)
        g_ref[:, HK * HD:] = acc_scr[part, HK * HD:].astype(BF16)


def query_kernel(n_lens, *refs):
    lens_refs, refs = refs[:n_lens], refs[n_lens:]
    q_ref, d_ref, kv0_ref, kv1_ref, kv2_ref, kv3_ref, final_ref, dq_ref, own_ref = refs[:9]
    starts_scr, bias_scr, kt_scr, s_scr, dp_scr, ds_scr, w_scr = refs[9:]
    rows = q_ref.shape[0]
    refs = [kv0_ref, kv1_ref, kv2_ref, kv3_ref]
    fill_bias(lens_refs, starts_scr, bias_scr, (0,) + offsets_of_moved(), rows)
    own_ref[...] = jnp.zeros_like(own_ref)
    for group in range(HK):
        for b, ref in enumerate(refs):
            kt_scr[group, :, b * rows:(b + 1) * rows] = ref[:, group * HD:(group + 1) * HD].T

    def first(i, slot):
        s_scr[slot] = scores_of(refs, q_ref, bias_scr, i)
        dp_scr[slot] = dweights_of(refs, d_ref, i)

    def second(i, slot):
        column = at(i, 2 * rows)
        p = jnp.exp((s_scr[slot] - final_ref[0:1, column]) * SCALE)
        w = p * final_ref[1:2, column]
        ds_scr[slot] = (w * (dp_scr[slot] - final_ref[2:3, column])).astype(BF16)
        w_scr[slot] = w[:rows].astype(BF16)

    def third(i, slot):
        group = i // SLOTS
        own_ref[:, at(group, HD)] += SCALE * lax.dot_general(
            ds_scr[slot, :rows], stacked(q_ref, i), NN, preferred_element_type=F32
        )
        own_ref[:, at(HK + group, HD)] += lax.dot_general(
            w_scr[slot], stacked(d_ref, i), NN, preferred_element_type=F32
        )
        dqt = lax.dot_general(kt_scr[group], ds_scr[slot], NN, preferred_element_type=F32)
        dq = (dqt * SCALE).astype(BF16).T
        dq_ref[:, at(2 * i, HD)] = dq[:rows]
        dq_ref[:, at(2 * i + 1, HD)] = dq[rows:]

    pipelined([first, second, third])


def call(body, lens, args, outs, scratch, matmul_rows, grant):
    specs = [pl.BlockSpec(memory_space=pltpu.SMEM)] * len(lens)
    specs += [pl.BlockSpec(memory_space=pltpu.VMEM)] * len(args)
    docs = sum(x.shape[0] for x in lens)
    return pl.pallas_call(
        functools.partial(body, len(lens)),
        in_specs=specs,
        out_specs=[pl.BlockSpec(memory_space=pltpu.VMEM)] * len(outs),
        out_shape=outs,
        scratch_shapes=[pltpu.SMEM((docs,), jnp.int32)] + scratch,
        cost_estimate=pl.CostEstimate(
            flops=2 * HQ * HD * HD * matmul_rows,
            bytes_accessed=sum(x.size * x.dtype.itemsize for x in list(args) + list(outs)),
            transcendentals=0,
        ),
        compiler_params=pltpu.CompilerParams(vmem_limit_bytes=grant << 20),
    )(*lens, *args)


def on_device(queries, keys_values, out_grads, doc_lengths):
    kv, q, dout = keys_values[0], queries[0], out_grads[0]
    rows, wide = kv.shape
    array = jax.ShapeDtypeStruct
    stat = array((8, HQ * rows), F32)
    blocks = REACH * rows
    keys = blocks + rows
    near = one_three(kv)
    far = three_one(kv)
    lens = all_lengths(doc_lengths)
    side = swapped(near)
    (stats,) = call(
        own_stats_kernel, lens, (q, dout, kv), [stat],
        [pltpu.VMEM((rows, rows), F32)] + [pltpu.VMEM((SLOTS, rows, 2 * rows), F32)] * 2,
        2 * rows, 8,
    )
    final, g_near, g_side, g_far = call(
        moved_kernel, lens, (q, dout, near, side, far, stats),
        [stat] + [array((rows, wide), BF16)] * 3,
        [pltpu.VMEM((blocks, rows), F32)]
        + [pltpu.VMEM((SLOTS, blocks, 2 * rows), F32)] * 3
        + [pltpu.VMEM((SLOTS, 8, 2 * rows), F32), pltpu.VMEM((blocks, wide), F32)],
        4 * blocks, 20,
    )
    back = three_one_back(g_far)
    side_back = swapped(g_side)
    joined = (g_near.astype(F32) + side_back.astype(F32)).astype(BF16)
    near_back = one_three_back(joined)
    dq, own = call(
        query_kernel, lens, (q, dout, kv, near, side, far, final),
        [array(q.shape, BF16), array((rows, wide), F32)],
        [pltpu.VMEM((keys, rows), F32), pltpu.VMEM((HK, HD, keys), BF16)]
        + [pltpu.VMEM((SLOTS, keys, 2 * rows), F32)] * 2
        + [pltpu.VMEM((SLOTS, keys, 2 * rows), BF16)]
        + [pltpu.VMEM((SLOTS, rows, 2 * rows), BF16)],
        4 * keys, 20,
    )
    total = own + back.astype(F32) + near_back.astype(F32)
    return (dq[None], total.astype(BF16)[None])


def solution(mesh):
    spec = P("pipe", "ctx", None)
    return jax.shard_map(
        on_device,
        mesh=mesh,
        in_specs=(spec, spec, spec, P("pipe")),
        out_specs=(spec, spec),
        check_vma=False,
    )
```

```python
import functools
import math

import jax
import jax.numpy as jnp
from jax import lax
from jax.experimental import pallas as pl
from jax.experimental.pallas import tpu as pltpu
from jax.sharding import PartitionSpec as P


HQ = 32
HK = 4
HD = 128
REACH = 3
GROUP = HQ // HK
F32 = jnp.float32
BF16 = jnp.bfloat16
NT = (((1,), (1,)), ((), ()))
NN = (((1,), (0,)), ((), ()))
SCALE = 1.0 / math.sqrt(HD)
RATE = SCALE * math.log2(math.e)
PAIRS = HQ // 2
PER_GROUP = GROUP // 2
SLOTS = 4


def moved(value, target_of):
    count = lax.axis_size("ctx")
    pairs = [(i, target_of(i)) for i in range(count)]
    return lax.ppermute(value, "ctx", [(s, t) for s, t in pairs if 0 <= t < count])


def one_three(value):
    return moved(value, lambda i: i + 1 if i % 2 else i + 3)


def three_one(value):
    return moved(value, lambda i: i + 3 if i % 2 else i + 1)


def swapped(value):
    return moved(value, lambda i: i ^ 1)


def all_lengths(lengths):
    count = lax.axis_size("pipe")
    pieces, stride = [lengths], 1
    while stride < count:
        pieces.append(
            lax.ppermute(jnp.concatenate(pieces), "pipe", [(i, i ^ stride) for i in range(count)])
        )
        stride *= 2
    return pieces


def fill_bias(lens_refs, starts_scr, bias_scr, offsets, rows, base=None):
    here = lax.axis_index("ctx")
    pipe = lax.axis_index("pipe")
    t_pos = here * rows + lax.broadcasted_iota(jnp.int32, (1, rows), 1)
    per_pipe = lens_refs[0].shape[0]
    place = 0
    for ref in lens_refs:
        for k in range(ref.shape[0]):
            starts_scr[((place // per_pipe) ^ pipe) * per_pipe + place % per_pipe] = ref[k]
            place += 1

    def step(d, carry):
        start, doc_start = carry
        doc_start = jnp.where(t_pos >= start, start, doc_start)
        return start + starts_scr[d], doc_start

    _, doc_start = lax.fori_loop(0, place, step, (jnp.int32(0), jnp.zeros((1, rows), jnp.int32)))
    for b, offset in enumerate(offsets):
        u_pos = (here - offset) * rows + lax.broadcasted_iota(jnp.int32, (rows, rows), 0)
        kept = 0.0 if base is None else base
        bias_scr[at(b, rows)] = jnp.where(u_pos >= doc_start, kept, -1e30).astype(F32)


def offsets_of_moved():
    odd = lax.rem(lax.axis_index("ctx"), 2)
    return (1 + 2 * odd, 2, 3 - 2 * odd)


def at(i, width):
    return slice(i * width, (i + 1) * width)


def stacked(ref, first, count):
    return jnp.concatenate([ref[:, at(first + k, HD)] for k in range(count)], axis=0)


def tall(refs, column):
    return jnp.concatenate([ref[:, at(column, HD)] for ref in refs], axis=0)


def keys_of(refs, i):
    return tall(refs, i // PER_GROUP)


def values_of(refs, i):
    return tall(refs, HK + i // PER_GROUP)


def scores_of(refs, q_ref, bias_scr, i):
    s = lax.dot_general(keys_of(refs, i), stacked(q_ref, 2 * i, 2), NT, preferred_element_type=F32)
    bias = bias_scr[...]
    return s + jnp.concatenate([bias, bias], axis=1)


def dweights_of(refs, d_ref, i):
    return lax.dot_general(values_of(refs, i), stacked(d_ref, 2 * i, 2), NT, preferred_element_type=F32)


def pipelined(stages):
    for step in range(PAIRS + len(stages) - 1):
        for k, stage in enumerate(stages):
            if 0 <= step - k < PAIRS:
                stage(step - k)


def at_group_end(action):
    def stage(i):
        if i % PER_GROUP == PER_GROUP - 1:
            action(i // PER_GROUP)

    return stage


def exponentials_kernel(n_lens, n_blocks, offsets_of, *refs):
    lens_refs, refs = refs[:n_lens], refs[n_lens:]
    q_ref, d_ref = refs[:2]
    kv_refs, (stats_ref, p_ref, dp_ref) = refs[2:2 + n_blocks], refs[2 + n_blocks:5 + n_blocks]
    starts_scr, bias_scr, s_scr = refs[5 + n_blocks:]
    rows = q_ref.shape[0]
    fill_bias(lens_refs, starts_scr, bias_scr, offsets_of(), rows)

    def first(i):
        s_scr[i % SLOTS] = scores_of(kv_refs, q_ref, bias_scr, i)
        dp_ref[:, at(i, 2 * rows)] = dweights_of(kv_refs, d_ref, i)

    def second(i):
        column = at(i, 2 * rows)
        s = s_scr[i % SLOTS]
        top = jnp.max(s, axis=0, keepdims=True)
        p = jnp.exp2((s - top) * RATE)
        p_ref[:, column] = p
        stats_ref[0:1, column] = top
        stats_ref[1:2, column] = jnp.sum(p, axis=0, keepdims=True)
        stats_ref[2:3, column] = jnp.sum(p * dp_ref[:, column], axis=0, keepdims=True)

    pipelined([first, second])


def products_kernel(
    n_lens, q_hbm, d_hbm, kv_hbm, s_ref, dp_ref, q_ref, d_ref, kv_ref, sems, kv_sem
):
    rows = q_ref.shape[0]
    kv_copy = pltpu.make_async_copy(kv_hbm, kv_ref, kv_sem)
    kv_copy.start()
    copies = []
    for group in range(HK):
        part = at(group, GROUP * HD)
        for k, (source, target) in enumerate(((q_hbm, q_ref), (d_hbm, d_ref))):
            copies.append(
                pltpu.make_async_copy(source.at[:, part], target.at[:, part], sems.at[k, group])
            )
            copies[-1].start()
    kv_copy.wait()
    for i in range(PAIRS):
        if i % PER_GROUP == 0:
            for k in range(2):
                copies[2 * (i // PER_GROUP) + k].wait()
        column = at(i, 2 * rows)
        s_ref[:, column] = lax.dot_general(
            keys_of([kv_ref], i), stacked(q_ref, 2 * i, 2), NT, preferred_element_type=F32
        )
        dp_ref[:, column] = dweights_of([kv_ref], d_ref, i)


def causal_kernel(n_lens, causal_ref):
    u = lax.broadcasted_iota(jnp.int32, causal_ref.shape, 0)
    t = lax.broadcasted_iota(jnp.int32, causal_ref.shape, 1)
    causal_ref[...] = jnp.where(u <= t, 0.0, -1e30).astype(F32)


def own_kernel(n_lens, *refs):
    lens_refs, refs = refs[:n_lens], refs[n_lens:]
    s_ref, dp_ref, causal_ref, stats_ref, p_ref, starts_scr, bias_scr = refs
    rows = s_ref.shape[0]
    fill_bias(lens_refs, starts_scr, bias_scr, (0,), rows, causal_ref[...])
    for i in range(PAIRS):
        column = at(i, 2 * rows)
        s = s_ref[:, column] + jnp.concatenate([bias_scr[...]] * 2, axis=1)
        top = jnp.max(s, axis=0, keepdims=True)
        p = jnp.exp2((s - top) * RATE)
        p_ref[:, column] = p
        stats_ref[0:1, column] = top
        stats_ref[1:2, column] = jnp.sum(p, axis=0, keepdims=True)
        stats_ref[2:3, column] = jnp.sum(p * dp_ref[:, column], axis=0, keepdims=True)


def remote_kernel(n_lens, *refs):
    lens_refs, refs = refs[:n_lens], refs[n_lens:]
    q_ref, d_ref, kv_ref, own_ref, mid_ref, pm_ref, dpm_ref = refs[:7]
    final_ref, ds_ref, g1_ref, g2_ref, g3_ref = refs[7:12]
    starts_scr, bias_scr, s_scr, dp_scr, p_scr, row_scr, w_scr = refs[12:]
    rows = q_ref.shape[0]
    mid = pm_ref.shape[0]
    g_refs = (g1_ref, g2_ref, g3_ref)
    fill_bias(lens_refs, starts_scr, bias_scr, offsets_of_moved()[2:], rows)

    def first(i):
        s_scr[i % SLOTS] = scores_of([kv_ref], q_ref, bias_scr, i)
        dp_scr[i % SLOTS] = dweights_of([kv_ref], d_ref, i)

    def second(i):
        column = at(i, 2 * rows)
        s, dp = s_scr[i % SLOTS], dp_scr[i % SLOTS]
        own_top, mid_top = own_ref[0:1, column], mid_ref[0:1, column]
        top = jnp.maximum(jnp.max(s, axis=0, keepdims=True), jnp.maximum(own_top, mid_top))
        p = jnp.exp2((s - top) * RATE)
        p_scr[i % SLOTS] = p
        own = jnp.exp2((own_top - top) * RATE)
        other = jnp.exp2((mid_top - top) * RATE)
        total = own_ref[1:2, column] * own + mid_ref[1:2, column] * other
        dot = own_ref[2:3, column] * own + mid_ref[2:3, column] * other
        inv = 1.0 / (total + jnp.sum(p, axis=0, keepdims=True))
        delta = (dot + jnp.sum(p * dp, axis=0, keepdims=True)) * inv
        row_scr[i % SLOTS, 0:1] = other * inv
        row_scr[i % SLOTS, 1:2] = inv
        row_scr[i % SLOTS, 2:3] = delta
        final_ref[0:1, column] = own * inv
        final_ref[1:2, column] = delta

    def third(i):
        column = at(i, 2 * rows)
        half, part = i // PER_GROUP % 2, at(i % PER_GROUP, 2 * rows)
        delta = row_scr[i % SLOTS, 2:3]
        w = pm_ref[:, column] * row_scr[i % SLOTS, 0:1]
        ds_ref[:mid, column] = (w * (dpm_ref[:, column] - delta)).astype(BF16)
        w_scr[half, :mid, part] = w.astype(BF16)
        w = p_scr[i % SLOTS] * row_scr[i % SLOTS, 1:2]
        ds_ref[mid:, column] = (w * (dp_scr[i % SLOTS] - delta)).astype(BF16)
        w_scr[half, mid:, part] = w.astype(BF16)

    def key_grads(group):
        dk = SCALE * lax.dot_general(
            ds_ref[:, at(group, GROUP * rows)], stacked(q_ref, group * GROUP, GROUP), NN,
            preferred_element_type=F32,
        )
        for b, g_ref in enumerate(g_refs):
            g_ref[:, at(group, HD)] = dk[at(b, rows)].astype(BF16)

    def value_grads(group):
        dv = lax.dot_general(
            w_scr[group % 2], stacked(d_ref, group * GROUP, GROUP), NN, preferred_element_type=F32
        )
        for b, g_ref in enumerate(g_refs):
            g_ref[:, at(HK + group, HD)] = dv[at(b, rows)].astype(BF16)

    pipelined([first, second, third, at_group_end(key_grads), at_group_end(value_grads)])


def join_kernel(n_lens, a_ref, b_ref, c_ref, sum_ref):
    total = a_ref[...].astype(F32) + b_ref[...].astype(F32) + c_ref[...].astype(F32)
    sum_ref[...] = total.astype(BF16)


def query_kernel(n_lens, *refs):
    q_ref, d_ref, kv0_ref, kv1_ref, kv2_ref, kv3_ref = refs[:6]
    p_ref, dp_ref, final_ref, ds_ref, dq_ref, own_ref, kt_scr, ds_scr, w_scr = refs[6:]
    rows = q_ref.shape[0]
    kv_refs = [kv0_ref, kv1_ref, kv2_ref, kv3_ref]

    def first(i):
        group = i // PER_GROUP
        if i % PER_GROUP == 0:
            for b, ref in enumerate(kv_refs):
                kt_scr[group, :, at(b, rows)] = ref[:, at(group, HD)].T
        column = at(i, 2 * rows)
        half, part = group % 2, at(i % PER_GROUP, 2 * rows)
        w = p_ref[:, column] * final_ref[0:1, column]
        ds_scr[half, :, part] = (w * (dp_ref[:, column] - final_ref[1:2, column])).astype(BF16)
        w_scr[half, :, part] = w.astype(BF16)

    def second(i):
        half, part = i // PER_GROUP % 2, at(i % PER_GROUP, 2 * rows)
        ds = jnp.concatenate([ds_scr[half, :, part], ds_ref[:, at(i, 2 * rows)]], axis=0)
        dqt = lax.dot_general(kt_scr[i // PER_GROUP], ds, NN, preferred_element_type=F32)
        dq = (dqt * SCALE).astype(BF16).T
        dq_ref[:, at(2 * i, HD)] = dq[:rows]
        dq_ref[:, at(2 * i + 1, HD)] = dq[rows:]

    def own_grads(group):
        own_ref[:, at(group, HD)] = SCALE * lax.dot_general(
            ds_scr[group % 2], stacked(q_ref, group * GROUP, GROUP), NN, preferred_element_type=F32
        )
        own_ref[:, at(HK + group, HD)] = lax.dot_general(
            w_scr[group % 2], stacked(d_ref, group * GROUP, GROUP), NN, preferred_element_type=F32
        )

    pipelined([first, second, at_group_end(own_grads)])


def call(body, lens, args, outs, scratch, matmul_rows, grant, in_hbm=0):
    specs = [pl.BlockSpec(memory_space=pltpu.SMEM)] * len(lens)
    specs += [pl.BlockSpec(memory_space=pltpu.HBM)] * in_hbm
    specs += [pl.BlockSpec(memory_space=pltpu.VMEM)] * (len(args) - in_hbm)
    docs = sum(x.shape[0] for x in lens)
    return pl.pallas_call(
        functools.partial(body, len(lens)),
        in_specs=specs,
        out_specs=[pl.BlockSpec(memory_space=pltpu.VMEM)] * len(outs),
        out_shape=outs,
        scratch_shapes=([pltpu.SMEM((docs,), jnp.int32)] if lens else []) + scratch,
        cost_estimate=pl.CostEstimate(
            flops=2 * HQ * HD * HD * matmul_rows,
            bytes_accessed=sum(x.size * x.dtype.itemsize for x in list(args) + list(outs)),
            transcendentals=0,
        ),
        compiler_params=pltpu.CompilerParams(vmem_limit_bytes=grant << 20),
    )(*lens, *args)


def exponentials(lens, q, dout, kvs, offsets_of):
    rows = q.shape[0]
    tall_rows = len(kvs) * rows
    array = jax.ShapeDtypeStruct
    return call(
        lambda n_lens, *refs: exponentials_kernel(n_lens, len(kvs), offsets_of, *refs),
        lens, (q, dout) + tuple(kvs),
        [array((8, HQ * rows), F32)] + [array((tall_rows, HQ * rows), F32)] * 2,
        [pltpu.VMEM((tall_rows, rows), F32), pltpu.VMEM((SLOTS, tall_rows, 2 * rows), F32)],
        2 * tall_rows, 4,
    )


def on_device(queries, keys_values, out_grads, doc_lengths):
    kv, q, dout = keys_values[0], queries[0], out_grads[0]
    rows, wide = kv.shape
    array = jax.ShapeDtypeStruct
    blocks = REACH * rows
    keys = blocks + rows
    near = one_three(kv)
    far = three_one(kv)
    lens = all_lengths(doc_lengths)
    side = swapped(near)
    square = array((rows, HQ * rows), F32)
    (causal,) = call(causal_kernel, (), (), [array((rows, rows), F32)], [], keys, 1)
    s_own, dp_own, q, dout, kv = call(
        products_kernel, (),
        [pltpu.with_memory_space_constraint(x, pltpu.HBM) for x in (q, dout, kv)],
        [square, square] + [array(x.shape, BF16) for x in (q, dout, kv)],
        [pltpu.SemaphoreType.DMA((2, HK)), pltpu.SemaphoreType.DMA(())],
        2 * rows, 4, in_hbm=3,
    )
    own_stats, p_own = call(
        own_kernel, lens, (s_own, dp_own, causal),
        [array((8, HQ * rows), F32), square], [pltpu.VMEM((rows, rows), F32)], rows, 2,
    )
    mid_stats, p_mid, dp_mid = exponentials(
        lens, q, dout, (near, side), lambda: offsets_of_moved()[:2]
    )
    final, ds, g_near, g_side, g_far = call(
        remote_kernel, lens,
        (q, dout, far, own_stats, mid_stats, p_mid, dp_mid),
        [array((8, HQ * rows), F32), array((blocks, HQ * rows), BF16)]
        + [array((rows, wide), BF16)] * 3,
        [pltpu.VMEM((rows, rows), F32)]
        + [pltpu.VMEM((SLOTS, rows, 2 * rows), F32)] * 3
        + [pltpu.VMEM((SLOTS, 8, 2 * rows), F32)]
        + [pltpu.VMEM((2, blocks, GROUP * rows), BF16)],
        2 * rows + 2 * blocks, 8,
    )
    relayed = moved(g_far, lambda i: -1 if i % 2 else i - 2)
    side_back = swapped(g_side)
    chip_back = moved(g_far, lambda i: i - 1 if i % 2 else -1)
    joined = g_near.astype(F32) + side_back.astype(F32)
    odd_back = moved(joined.astype(BF16), lambda i: i - 3 if i % 2 else -1)
    dq, own = call(
        query_kernel, (),
        (q, dout, kv, near, side, far, p_own, dp_own, final, ds),
        [array(q.shape, BF16), array((rows, wide), F32)],
        [pltpu.VMEM((HK, HD, keys), BF16)]
        + [pltpu.VMEM((2, rows, GROUP * rows), BF16)] * 2,
        2 * rows + keys, 6,
    )
    (joined,) = call(
        join_kernel, (), (g_near, side_back, relayed),
        [array((rows, wide), BF16)], [], 1, 1,
    )
    even_back = moved(joined, lambda i: -1 if i % 2 else i - 1)
    total = own + chip_back.astype(F32) + odd_back.astype(F32) + even_back.astype(F32)
    return (dq[None], total.astype(BF16)[None])


def solution(mesh):
    spec = P("pipe", "ctx", None)
    return jax.shard_map(
        on_device,
        mesh=mesh,
        in_specs=(spec, spec, spec, P("pipe")),
        out_specs=(spec, spec),
        check_vma=False,
    )
```

```python
import functools
import math

import jax
import jax.numpy as jnp
from jax import lax
from jax.experimental import pallas as pl
from jax.experimental.pallas import tpu as pltpu
from jax.sharding import PartitionSpec as P


HQ = 32
HK = 4
HD = 128
REACH = 3
GROUP = HQ // HK
F32 = jnp.float32
BF16 = jnp.bfloat16
NT = (((1,), (1,)), ((), ()))
NN = (((1,), (0,)), ((), ()))
SCALE = 1.0 / math.sqrt(HD)
RATE = SCALE * math.log2(math.e)
PAIRS = HQ // 2
PER_GROUP = GROUP // 2
SLOTS = 4


def moved(value, target_of):
    count = lax.axis_size("ctx")
    pairs = [(i, target_of(i)) for i in range(count)]
    return lax.ppermute(value, "ctx", [(s, t) for s, t in pairs if 0 <= t < count])


def one_three(value):
    return moved(value, lambda i: i + 1 if i % 2 else i + 3)


def three_one(value):
    return moved(value, lambda i: i + 3 if i % 2 else i + 1)


def swapped(value):
    return moved(value, lambda i: i ^ 1)


def all_lengths(lengths):
    count = lax.axis_size("pipe")
    pieces, stride = [lengths], 1
    while stride < count:
        pieces.append(
            lax.ppermute(jnp.concatenate(pieces), "pipe", [(i, i ^ stride) for i in range(count)])
        )
        stride *= 2
    return pieces


def fill_bias(lens_refs, starts_scr, bias_scr, offsets, rows, base=None):
    here = lax.axis_index("ctx")
    pipe = lax.axis_index("pipe")
    t_pos = here * rows + lax.broadcasted_iota(jnp.int32, (1, rows), 1)
    per_pipe = lens_refs[0].shape[0]
    place = 0
    for ref in lens_refs:
        for k in range(ref.shape[0]):
            starts_scr[((place // per_pipe) ^ pipe) * per_pipe + place % per_pipe] = ref[k]
            place += 1

    def step(d, carry):
        start, doc_start = carry
        doc_start = jnp.where(t_pos >= start, start, doc_start)
        return start + starts_scr[d], doc_start

    _, doc_start = lax.fori_loop(0, place, step, (jnp.int32(0), jnp.zeros((1, rows), jnp.int32)))
    for b, offset in enumerate(offsets):
        u_pos = (here - offset) * rows + lax.broadcasted_iota(jnp.int32, (rows, rows), 0)
        kept = 0.0 if base is None else base
        bias_scr[at(b, rows)] = jnp.where(u_pos >= doc_start, kept, -1e30).astype(F32)


def offsets_of_moved():
    odd = lax.rem(lax.axis_index("ctx"), 2)
    return (1 + 2 * odd, 2, 3 - 2 * odd)


def at(i, width):
    return slice(i * width, (i + 1) * width)


def stacked(ref, first, count):
    return jnp.concatenate([ref[:, at(first + k, HD)] for k in range(count)], axis=0)


def tall(refs, column):
    return jnp.concatenate([ref[:, at(column, HD)] for ref in refs], axis=0)


def keys_of(refs, i):
    return tall(refs, i // PER_GROUP)


def values_of(refs, i):
    return tall(refs, HK + i // PER_GROUP)


def scores_of(refs, q_ref, bias_scr, i):
    s = lax.dot_general(keys_of(refs, i), stacked(q_ref, 2 * i, 2), NT, preferred_element_type=F32)
    bias = bias_scr[...]
    return s + jnp.concatenate([bias, bias], axis=1)


def dweights_of(refs, d_ref, i):
    return lax.dot_general(values_of(refs, i), stacked(d_ref, 2 * i, 2), NT, preferred_element_type=F32)


def pipelined(stages):
    for step in range(PAIRS + len(stages) - 1):
        for k, stage in enumerate(stages):
            if 0 <= step - k < PAIRS:
                stage(step - k)


def at_group_end(action):
    def stage(i):
        if i % PER_GROUP == PER_GROUP - 1:
            action(i // PER_GROUP)

    return stage


def exponentials_kernel(n_lens, n_blocks, offsets_of, *refs):
    lens_refs, refs = refs[:n_lens], refs[n_lens:]
    q_ref, d_ref = refs[:2]
    kv_refs, (stats_ref, p_ref, dp_ref) = refs[2:2 + n_blocks], refs[2 + n_blocks:5 + n_blocks]
    starts_scr, bias_scr, s_scr = refs[5 + n_blocks:]
    rows = q_ref.shape[0]
    fill_bias(lens_refs, starts_scr, bias_scr, offsets_of(), rows)

    def first(i):
        s_scr[i % SLOTS] = scores_of(kv_refs, q_ref, bias_scr, i)
        dp_ref[:, at(i, 2 * rows)] = dweights_of(kv_refs, d_ref, i)

    def second(i):
        column = at(i, 2 * rows)
        s = s_scr[i % SLOTS]
        top = jnp.max(s, axis=0, keepdims=True)
        p = jnp.exp2((s - top) * RATE)
        p_ref[:, column] = p
        stats_ref[0:1, column] = top
        stats_ref[1:2, column] = jnp.sum(p, axis=0, keepdims=True)
        stats_ref[2:3, column] = jnp.sum(p * dp_ref[:, column], axis=0, keepdims=True)

    pipelined([first, second])


def products_kernel(n_lens, q_ref, d_ref, kv_ref, s_ref, dp_ref):
    rows = q_ref.shape[0]
    for i in range(PAIRS):
        column = at(i, 2 * rows)
        s_ref[:, column] = lax.dot_general(
            keys_of([kv_ref], i), stacked(q_ref, 2 * i, 2), NT, preferred_element_type=F32
        )
        dp_ref[:, column] = dweights_of([kv_ref], d_ref, i)


def causal_kernel(n_lens, causal_ref):
    u = lax.broadcasted_iota(jnp.int32, causal_ref.shape, 0)
    t = lax.broadcasted_iota(jnp.int32, causal_ref.shape, 1)
    causal_ref[...] = jnp.where(u <= t, 0.0, -1e30).astype(F32)


def own_kernel(n_lens, *refs):
    lens_refs, refs = refs[:n_lens], refs[n_lens:]
    s_ref, dp_ref, causal_ref, stats_ref, p_ref, starts_scr, bias_scr = refs
    rows = s_ref.shape[0]
    fill_bias(lens_refs, starts_scr, bias_scr, (0,), rows, causal_ref[...])
    for i in range(PAIRS):
        column = at(i, 2 * rows)
        s = s_ref[:, column] + jnp.concatenate([bias_scr[...]] * 2, axis=1)
        top = jnp.max(s, axis=0, keepdims=True)
        p = jnp.exp2((s - top) * RATE)
        p_ref[:, column] = p
        stats_ref[0:1, column] = top
        stats_ref[1:2, column] = jnp.sum(p, axis=0, keepdims=True)
        stats_ref[2:3, column] = jnp.sum(p * dp_ref[:, column], axis=0, keepdims=True)


def far_kernel(n_lens, *refs):
    lens_refs, refs = refs[:n_lens], refs[n_lens:]
    q_ref, d_ref, kv_ref, own_ref, mid_ref = refs[:5]
    final_ref, ds_ref, g_ref = refs[5:8]
    starts_scr, bias_scr, s_scr, dp_scr, p_scr, row_scr, w_scr = refs[8:]
    rows = q_ref.shape[0]
    fill_bias(lens_refs, starts_scr, bias_scr, offsets_of_moved()[2:], rows)

    def first(i):
        s_scr[i % SLOTS] = scores_of([kv_ref], q_ref, bias_scr, i)
        dp_scr[i % SLOTS] = dweights_of([kv_ref], d_ref, i)

    def second(i):
        column = at(i, 2 * rows)
        s, dp = s_scr[i % SLOTS], dp_scr[i % SLOTS]
        own_top, mid_top = own_ref[0:1, column], mid_ref[0:1, column]
        top = jnp.maximum(jnp.max(s, axis=0, keepdims=True), jnp.maximum(own_top, mid_top))
        p = jnp.exp2((s - top) * RATE)
        p_scr[i % SLOTS] = p
        own = jnp.exp2((own_top - top) * RATE)
        other = jnp.exp2((mid_top - top) * RATE)
        total = own_ref[1:2, column] * own + mid_ref[1:2, column] * other
        dot = own_ref[2:3, column] * own + mid_ref[2:3, column] * other
        inv = 1.0 / (total + jnp.sum(p, axis=0, keepdims=True))
        delta = (dot + jnp.sum(p * dp, axis=0, keepdims=True)) * inv
        row_scr[i % SLOTS, 0:1] = inv
        row_scr[i % SLOTS, 1:2] = delta
        final_ref[0:1, column] = own * inv
        final_ref[1:2, column] = delta
        final_ref[2:3, column] = other * inv

    def third(i):
        w = p_scr[i % SLOTS] * row_scr[i % SLOTS, 0:1]
        ds = (w * (dp_scr[i % SLOTS] - row_scr[i % SLOTS, 1:2])).astype(BF16)
        ds_ref[:, at(i, 2 * rows)] = ds
        w_scr[i // PER_GROUP % 2, :, at(i % PER_GROUP, 2 * rows)] = w.astype(BF16)

    def gradients(group):
        dk = lax.dot_general(
            ds_ref[:, at(group, GROUP * rows)], stacked(q_ref, group * GROUP, GROUP), NN,
            preferred_element_type=F32,
        )
        g_ref[:, at(group, HD)] = (dk * SCALE).astype(BF16)
        dv = lax.dot_general(
            w_scr[group % 2], stacked(d_ref, group * GROUP, GROUP), NN, preferred_element_type=F32
        )
        g_ref[:, at(HK + group, HD)] = dv.astype(BF16)

    pipelined([first, second, third, at_group_end(gradients)])


def mid_kernel(n_lens, *refs):
    q_ref, d_ref, p_ref, dp_ref, final_ref, far_ref, near_ref, pair_ref, ds_ref, w_scr = refs
    rows = q_ref.shape[0]
    pair_ref[rows:] = far_ref[...]

    def first(i):
        column = at(i, 2 * rows)
        w = p_ref[:, column] * final_ref[2:3, column]
        ds_ref[:, column] = (w * (dp_ref[:, column] - final_ref[1:2, column])).astype(BF16)
        w_scr[i // PER_GROUP % 2, :, at(i % PER_GROUP, 2 * rows)] = w.astype(BF16)

    def key_grads(group):
        dk = lax.dot_general(
            ds_ref[:, at(group, GROUP * rows)], stacked(q_ref, group * GROUP, GROUP), NN,
            preferred_element_type=F32,
        )
        dk = (dk * SCALE).astype(BF16)
        near_ref[:, at(group, HD)] = dk[:rows]
        pair_ref[:rows, at(group, HD)] = dk[rows:]

    def value_grads(group):
        dv = lax.dot_general(
            w_scr[group % 2], stacked(d_ref, group * GROUP, GROUP), NN, preferred_element_type=F32
        ).astype(BF16)
        near_ref[:, at(HK + group, HD)] = dv[:rows]
        pair_ref[:rows, at(HK + group, HD)] = dv[rows:]

    pipelined([first, at_group_end(key_grads), at_group_end(value_grads)])


def sum_kernel(n_lens, near_ref, pair_ref, *refs):
    rows = near_ref.shape[0]
    total = near_ref[...].astype(F32) + pair_ref[:rows].astype(F32)
    for ref in refs[:-1]:
        total = total + ref[...].astype(F32)
    refs[-1][...] = total.astype(BF16)


def finish_kernel(n_lens, own_ref, pair_ref, odd_ref, even_ref, total_ref):
    rows = own_ref.shape[0]
    even = lax.rem(lax.axis_index("ctx"), 2) == 0
    chip = pair_ref[rows:].astype(F32) + odd_ref[...].astype(F32)
    moved_in = jnp.where(even, chip, even_ref[...].astype(F32))
    total_ref[...] = (own_ref[...] + moved_in).astype(BF16)


def query_kernel(n_lens, *refs):
    q_ref, d_ref, kv0_ref, kv1_ref, kv2_ref, kv3_ref = refs[:6]
    p_ref, dp_ref, final_ref, mid_ref, far_ref, dq_ref, own_ref, kt_scr, ds_scr, w_scr = refs[6:]
    rows = q_ref.shape[0]
    kv_refs = [kv0_ref, kv1_ref, kv2_ref, kv3_ref]

    def first(i):
        group = i // PER_GROUP
        if i % PER_GROUP == 0:
            for b, ref in enumerate(kv_refs):
                kt_scr[group, :, at(b, rows)] = ref[:, at(group, HD)].T
        column = at(i, 2 * rows)
        half, part = group % 2, at(i % PER_GROUP, 2 * rows)
        w = p_ref[:, column] * final_ref[0:1, column]
        ds_scr[half, :, part] = (w * (dp_ref[:, column] - final_ref[1:2, column])).astype(BF16)
        w_scr[half, :, part] = w.astype(BF16)

    def second(i):
        half, part = i // PER_GROUP % 2, at(i % PER_GROUP, 2 * rows)
        column = at(i, 2 * rows)
        ds = jnp.concatenate(
            [ds_scr[half, :, part], mid_ref[:, column], far_ref[:, column]], axis=0
        )
        dqt = lax.dot_general(kt_scr[i // PER_GROUP], ds, NN, preferred_element_type=F32)
        dq = (dqt * SCALE).astype(BF16).T
        dq_ref[:, at(2 * i, HD)] = dq[:rows]
        dq_ref[:, at(2 * i + 1, HD)] = dq[rows:]

    def own_grads(group):
        own_ref[:, at(group, HD)] = SCALE * lax.dot_general(
            ds_scr[group % 2], stacked(q_ref, group * GROUP, GROUP), NN, preferred_element_type=F32
        )
        own_ref[:, at(HK + group, HD)] = lax.dot_general(
            w_scr[group % 2], stacked(d_ref, group * GROUP, GROUP), NN, preferred_element_type=F32
        )

    pipelined([first, second, at_group_end(own_grads)])


def call(body, lens, args, outs, scratch, matmul_rows, grant):
    specs = [pl.BlockSpec(memory_space=pltpu.SMEM)] * len(lens)
    specs += [pl.BlockSpec(memory_space=pltpu.VMEM)] * len(args)
    docs = sum(x.shape[0] for x in lens)
    return pl.pallas_call(
        functools.partial(body, len(lens)),
        in_specs=specs,
        out_specs=[pl.BlockSpec(memory_space=pltpu.VMEM)] * len(outs),
        out_shape=outs,
        scratch_shapes=([pltpu.SMEM((docs,), jnp.int32)] if lens else []) + scratch,
        cost_estimate=pl.CostEstimate(
            flops=2 * HQ * HD * HD * matmul_rows,
            bytes_accessed=sum(x.size * x.dtype.itemsize for x in list(args) + list(outs)),
            transcendentals=0,
        ),
        compiler_params=pltpu.CompilerParams(vmem_limit_bytes=grant << 20),
    )(*lens, *args)


def exponentials(lens, q, dout, kvs, offsets_of):
    rows = q.shape[0]
    tall_rows = len(kvs) * rows
    array = jax.ShapeDtypeStruct
    return call(
        lambda n_lens, *refs: exponentials_kernel(n_lens, len(kvs), offsets_of, *refs),
        lens, (q, dout) + tuple(kvs),
        [array((8, HQ * rows), F32)] + [array((tall_rows, HQ * rows), F32)] * 2,
        [pltpu.VMEM((tall_rows, rows), F32), pltpu.VMEM((SLOTS, tall_rows, 2 * rows), F32)],
        2 * tall_rows, 4,
    )


def on_device(queries, keys_values, out_grads, doc_lengths):
    kv, q, dout = keys_values[0], queries[0], out_grads[0]
    rows, wide = kv.shape
    array = jax.ShapeDtypeStruct
    blocks = REACH * rows
    keys = blocks + rows
    near = one_three(kv)
    far = three_one(kv)
    lens = all_lengths(doc_lengths)
    side = swapped(near)
    square = array((rows, HQ * rows), F32)
    (causal,) = call(causal_kernel, (), (), [array((rows, rows), F32)], [], 100 * keys, 1)
    s_own, dp_own = call(products_kernel, (), (q, dout, kv), [square, square], [], 2 * rows, 4)
    own_stats, p_own = call(
        own_kernel, lens, (s_own, dp_own, causal),
        [array((8, HQ * rows), F32), square], [pltpu.VMEM((rows, rows), F32)], rows, 2,
    )
    mid_stats, p_mid, dp_mid = exponentials(
        lens, q, dout, (near, side), lambda: offsets_of_moved()[:2]
    )
    final, ds_far, g_far = call(
        far_kernel, lens, (q, dout, far, own_stats, mid_stats),
        [array((8, HQ * rows), F32), array((rows, HQ * rows), BF16), array((rows, wide), BF16)],
        [pltpu.VMEM((rows, rows), F32)]
        + [pltpu.VMEM((SLOTS, rows, 2 * rows), F32)] * 3
        + [pltpu.VMEM((SLOTS, 8, 2 * rows), F32)]
        + [pltpu.VMEM((2, rows, GROUP * rows), BF16)],
        4 * rows, 6,
    )
    relayed = moved(g_far, lambda i: -1 if i % 2 else i - 2)
    g_near, g_pair, ds_mid = call(
        mid_kernel, (), (q, dout, p_mid, dp_mid, final, g_far),
        [
            array((rows, wide), BF16),
            array((2 * rows, wide), BF16),
            array((2 * rows, HQ * rows), BF16),
        ],
        [pltpu.VMEM((2, 2 * rows, GROUP * rows), BF16)], 4 * rows, 4,
    )
    pair_back = swapped(g_pair)
    block = array((rows, wide), BF16)
    (odd_sum,) = call(sum_kernel, (), (g_near, pair_back), [block], [], 1, 1)
    odd_back = moved(odd_sum, lambda i: i - 3 if i % 2 else -1)
    (joined,) = call(sum_kernel, (), (g_near, pair_back, relayed), [block], [], 1, 1)
    even_back = moved(joined, lambda i: -1 if i % 2 else i - 1)
    dq, own = call(
        query_kernel, (),
        (q, dout, kv, near, side, far, p_own, dp_own, final, ds_mid, ds_far),
        [array(q.shape, BF16), array((rows, wide), F32)],
        [pltpu.VMEM((HK, HD, keys), BF16)]
        + [pltpu.VMEM((2, rows, GROUP * rows), BF16)] * 2,
        2 * rows + keys, 6,
    )
    (total,) = call(finish_kernel, (), (own, pair_back, odd_back, even_back), [block], [], 1, 3)
    return (dq[None], total[None])


def solution(mesh):
    spec = P("pipe", "ctx", None)
    return jax.shard_map(
        on_device,
        mesh=mesh,
        in_specs=(spec, spec, spec, P("pipe")),
        out_specs=(spec, spec),
        check_vma=False,
    )
```

```python
import functools
import math

import jax
import jax.numpy as jnp
from jax import lax
from jax.experimental import pallas as pl
from jax.experimental.pallas import tpu as pltpu
from jax.sharding import PartitionSpec as P


HQ = 32
HK = 4
HD = 128
REACH = 3
GROUP = HQ // HK
F32 = jnp.float32
BF16 = jnp.bfloat16
NT = (((1,), (1,)), ((), ()))
NN = (((1,), (0,)), ((), ()))
SCALE = 1.0 / math.sqrt(HD)
RATE = SCALE * math.log2(math.e)
PAIRS = HQ // 2
PER_GROUP = GROUP // 2
SLOTS = 4


def moved(value, target_of):
    count = lax.axis_size("ctx")
    pairs = [(i, target_of(i)) for i in range(count)]
    return lax.ppermute(value, "ctx", [(s, t) for s, t in pairs if 0 <= t < count])


def one_three(value):
    return moved(value, lambda i: i + 1 if i % 2 else i + 3)


def three_one(value):
    return moved(value, lambda i: i + 3 if i % 2 else i + 1)


def swapped(value):
    return moved(value, lambda i: i ^ 1)


def all_lengths(lengths):
    count = lax.axis_size("pipe")
    pieces, stride = [lengths], 1
    while stride < count:
        pieces.append(
            lax.ppermute(jnp.concatenate(pieces), "pipe", [(i, i ^ stride) for i in range(count)])
        )
        stride *= 2
    return pieces


def positions(rows):
    return lax.axis_index("ctx") * rows + lax.broadcasted_iota(jnp.int32, (1, rows), 1)


def find_doc_starts(lens_refs, starts_scr, rows):
    pipe = lax.axis_index("pipe")
    t_pos = positions(rows)
    per_pipe = lens_refs[0].shape[0]
    place = 0
    for ref in lens_refs:
        for k in range(ref.shape[0]):
            starts_scr[((place // per_pipe) ^ pipe) * per_pipe + place % per_pipe] = ref[k]
            place += 1
    start, doc_start = jnp.int32(0), jnp.zeros((1, rows), jnp.int32)
    for d in range(place):
        doc_start = jnp.where(t_pos >= start, start, doc_start)
        start = start + starts_scr[d]
    return doc_start


def bias_of(doc_start, offset, base):
    rows = doc_start.shape[1]
    u_pos = (lax.axis_index("ctx") - offset) * rows
    u_pos = u_pos + lax.broadcasted_iota(jnp.int32, (rows, rows), 0)
    return jnp.where(u_pos >= doc_start, base, -1e30).astype(F32)


def is_odd():
    return lax.rem(lax.axis_index("ctx"), 2)


def at(i, width):
    return slice(i * width, (i + 1) * width)


def stacked(ref, first, count):
    return jnp.concatenate([ref[:, at(first + k, HD)] for k in range(count)], axis=0)


def scores_of(kv_ref, q_ref, i):
    return lax.dot_general(
        kv_ref[:, at(i // PER_GROUP, HD)], stacked(q_ref, 2 * i, 2), NT, preferred_element_type=F32
    )


def dweights_of(kv_ref, d_ref, i):
    return lax.dot_general(
        kv_ref[:, at(HK + i // PER_GROUP, HD)], stacked(d_ref, 2 * i, 2), NT,
        preferred_element_type=F32,
    )


def twice(value):
    return jnp.concatenate([value, value], axis=1)


def pipelined(stages):
    for step in range(PAIRS + len(stages) - 1):
        for k, stage in enumerate(stages):
            if 0 <= step - k < PAIRS:
                stage(step - k)


def at_group_end(action):
    def stage(i):
        if i % PER_GROUP == PER_GROUP - 1:
            action(i // PER_GROUP)

    return stage


def products_kernel(n_lens, q_ref, d_ref, kv_ref, s_ref, dp_ref):
    rows = q_ref.shape[0]
    for i in range(PAIRS):
        s_ref[:, at(i, 2 * rows)] = scores_of(kv_ref, q_ref, i)
        dp_ref[:, at(i, 2 * rows)] = dweights_of(kv_ref, d_ref, i)


def causal_kernel(n_lens, causal_ref):
    u = lax.broadcasted_iota(jnp.int32, causal_ref.shape, 0)
    t = lax.broadcasted_iota(jnp.int32, causal_ref.shape, 1)
    causal_ref[...] = jnp.where(u <= t, 0.0, -1e30).astype(F32)


def keep_exponentials(s, dp, column, stats_ref, p_ref):
    top = jnp.max(s, axis=0, keepdims=True)
    p = jnp.exp2((s - top) * RATE)
    p_ref[:, column] = p
    stats_ref[0:1, column] = top
    stats_ref[1:2, column] = jnp.sum(p, axis=0, keepdims=True)
    stats_ref[2:3, column] = jnp.sum(p * dp, axis=0, keepdims=True)


def own_kernel(n_lens, *refs):
    lens_refs, refs = refs[:n_lens], refs[n_lens:]
    s_ref, dp_ref, causal_ref, stats_ref, p_ref, docs_ref, starts_scr, bias_scr = refs
    rows = s_ref.shape[0]
    doc_start = find_doc_starts(lens_refs, starts_scr, rows)
    docs_ref[0:1] = doc_start
    bias_scr[...] = bias_of(doc_start, 0, causal_ref[...])
    for i in range(PAIRS):
        column = at(i, 2 * rows)
        s = s_ref[:, column] + twice(bias_scr[...])
        keep_exponentials(s, dp_ref[:, column], column, stats_ref, p_ref)


def block_kernel(offset_of, n_lens, *refs):
    docs_ref, q_ref, d_ref, kv_ref, stats_ref, p_ref, dp_ref, bias_scr, s_scr = refs
    rows = q_ref.shape[0]
    bias_scr[...] = bias_of(docs_ref[0:1], offset_of(), 0.0)

    def first(i):
        s_scr[i % SLOTS] = scores_of(kv_ref, q_ref, i) + twice(bias_scr[...])
        dp_ref[:, at(i, 2 * rows)] = dweights_of(kv_ref, d_ref, i)

    def second(i):
        column = at(i, 2 * rows)
        keep_exponentials(s_scr[i % SLOTS], dp_ref[:, column], column, stats_ref, p_ref)

    pipelined([first, second])


def far_kernel(n_lens, *refs):
    docs_ref, q_ref, d_ref, kv_ref = refs[:4]
    stats_refs = refs[4:7]
    final_ref, ds_ref, g_ref = refs[7:10]
    bias_scr, s_scr, dp_scr, p_scr, row_scr, w_scr = refs[10:]
    rows = q_ref.shape[0]
    bias_scr[...] = bias_of(docs_ref[0:1], 3 - 2 * is_odd(), 0.0)

    def first(i):
        s_scr[i % SLOTS] = scores_of(kv_ref, q_ref, i) + twice(bias_scr[...])
        dp_scr[i % SLOTS] = dweights_of(kv_ref, d_ref, i)

    def second(i):
        column = at(i, 2 * rows)
        s = s_scr[i % SLOTS]
        tops = [ref[0:1, column] for ref in stats_refs]
        top = functools.reduce(jnp.maximum, tops, jnp.max(s, axis=0, keepdims=True))
        p = jnp.exp2((s - top) * RATE)
        p_scr[i % SLOTS] = p
        total = jnp.sum(p, axis=0, keepdims=True)
        dot = jnp.sum(p * dp_scr[i % SLOTS], axis=0, keepdims=True)
        shares = [jnp.exp2((block_top - top) * RATE) for block_top in tops]
        for ref, share in zip(stats_refs, shares):
            total = total + ref[1:2, column] * share
            dot = dot + ref[2:3, column] * share
        inv = 1.0 / total
        delta = dot * inv
        row_scr[i % SLOTS, 0:1] = inv
        row_scr[i % SLOTS, 1:2] = delta
        final_ref[0:1, column] = delta
        for k, share in enumerate(shares):
            final_ref[k + 1:k + 2, column] = share * inv

    def third(i):
        w = p_scr[i % SLOTS] * row_scr[i % SLOTS, 0:1]
        ds = (w * (dp_scr[i % SLOTS] - row_scr[i % SLOTS, 1:2])).astype(BF16)
        ds_ref[:, at(i, 2 * rows)] = ds
        w_scr[i // PER_GROUP % 2, :, at(i % PER_GROUP, 2 * rows)] = w.astype(BF16)

    def gradients(group):
        dk = lax.dot_general(
            ds_ref[:, at(group, GROUP * rows)], stacked(q_ref, group * GROUP, GROUP), NN,
            preferred_element_type=F32,
        )
        g_ref[:, at(group, HD)] = (dk * SCALE).astype(BF16)
        dv = lax.dot_general(
            w_scr[group % 2], stacked(d_ref, group * GROUP, GROUP), NN, preferred_element_type=F32
        )
        g_ref[:, at(HK + group, HD)] = dv.astype(BF16)

    pipelined([first, second, third, at_group_end(gradients)])


def mid_kernel(n_lens, *refs):
    q_ref, d_ref, p1_ref, dp1_ref, p2_ref, dp2_ref, final_ref, far_ref = refs[:8]
    near_ref, pair_ref, ds_ref, w_scr = refs[8:]
    rows = q_ref.shape[0]
    pair_ref[rows:] = far_ref[...]

    def first(i):
        column = at(i, 2 * rows)
        for b, (p_ref, dp_ref) in enumerate(((p1_ref, dp1_ref), (p2_ref, dp2_ref))):
            w = p_ref[:, column] * final_ref[b + 2:b + 3, column]
            ds = (w * (dp_ref[:, column] - final_ref[0:1, column])).astype(BF16)
            ds_ref[at(b, rows), column] = ds
            w_scr[i // PER_GROUP % 2, at(b, rows), at(i % PER_GROUP, 2 * rows)] = w.astype(BF16)

    def key_grads(group):
        dk = lax.dot_general(
            ds_ref[:, at(group, GROUP * rows)], stacked(q_ref, group * GROUP, GROUP), NN,
            preferred_element_type=F32,
        )
        dk = (dk * SCALE).astype(BF16)
        near_ref[:, at(group, HD)] = dk[:rows]
        pair_ref[:rows, at(group, HD)] = dk[rows:]

    def value_grads(group):
        dv = lax.dot_general(
            w_scr[group % 2], stacked(d_ref, group * GROUP, GROUP), NN, preferred_element_type=F32
        ).astype(BF16)
        near_ref[:, at(HK + group, HD)] = dv[:rows]
        pair_ref[:rows, at(HK + group, HD)] = dv[rows:]

    pipelined([first, at_group_end(key_grads), at_group_end(value_grads)])


def sum_kernel(n_lens, near_ref, pair_ref, *refs):
    rows = near_ref.shape[0]
    total = near_ref[...].astype(F32) + pair_ref[:rows].astype(F32)
    for ref in refs[:-1]:
        total = total + ref[...].astype(F32)
    refs[-1][...] = total.astype(BF16)


def finish_kernel(n_lens, own_ref, pair_ref, odd_ref, even_ref, total_ref):
    rows = own_ref.shape[0]
    even = lax.rem(lax.axis_index("ctx"), 2) == 0
    chip = pair_ref[rows:].astype(F32) + odd_ref[...].astype(F32)
    moved_in = jnp.where(even, chip, even_ref[...].astype(F32))
    total_ref[...] = (own_ref[...] + moved_in).astype(BF16)


def query_kernel(n_lens, *refs):
    q_ref, d_ref, kv0_ref, kv1_ref, kv2_ref, kv3_ref = refs[:6]
    p_ref, dp_ref, final_ref, mid_ref, far_ref, dq_ref, own_ref, kt_scr, ds_scr, w_scr = refs[6:]
    rows = q_ref.shape[0]
    kv_refs = [kv0_ref, kv1_ref, kv2_ref, kv3_ref]

    def first(i):
        group = i // PER_GROUP
        if i % PER_GROUP == 0:
            for b, ref in enumerate(kv_refs):
                kt_scr[group, :, at(b, rows)] = ref[:, at(group, HD)].T
        column = at(i, 2 * rows)
        half, part = group % 2, at(i % PER_GROUP, 2 * rows)
        w = p_ref[:, column] * final_ref[1:2, column]
        ds_scr[half, :, part] = (w * (dp_ref[:, column] - final_ref[0:1, column])).astype(BF16)
        w_scr[half, :, part] = w.astype(BF16)

    def second(i):
        half, part = i // PER_GROUP % 2, at(i % PER_GROUP, 2 * rows)
        column = at(i, 2 * rows)
        ds = jnp.concatenate(
            [ds_scr[half, :, part], mid_ref[:, column], far_ref[:, column]], axis=0
        )
        dqt = lax.dot_general(kt_scr[i // PER_GROUP], ds, NN, preferred_element_type=F32)
        dq = (dqt * SCALE).astype(BF16).T
        dq_ref[:, at(2 * i, HD)] = dq[:rows]
        dq_ref[:, at(2 * i + 1, HD)] = dq[rows:]

    def own_grads(group):
        own_ref[:, at(group, HD)] = SCALE * lax.dot_general(
            ds_scr[group % 2], stacked(q_ref, group * GROUP, GROUP), NN, preferred_element_type=F32
        )
        own_ref[:, at(HK + group, HD)] = lax.dot_general(
            w_scr[group % 2], stacked(d_ref, group * GROUP, GROUP), NN, preferred_element_type=F32
        )

    pipelined([first, second, at_group_end(own_grads)])


def call(body, lens, args, outs, scratch, matmul_rows, grant):
    specs = [pl.BlockSpec(memory_space=pltpu.SMEM)] * len(lens)
    specs += [pl.BlockSpec(memory_space=pltpu.VMEM)] * len(args)
    docs = sum(x.shape[0] for x in lens)
    return pl.pallas_call(
        functools.partial(body, len(lens)),
        in_specs=specs,
        out_specs=[pl.BlockSpec(memory_space=pltpu.VMEM)] * len(outs),
        out_shape=outs,
        scratch_shapes=([pltpu.SMEM((docs,), jnp.int32)] if lens else []) + scratch,
        cost_estimate=pl.CostEstimate(
            flops=2 * HQ * HD * HD * matmul_rows,
            bytes_accessed=sum(x.size * x.dtype.itemsize for x in list(args) + list(outs)),
            transcendentals=0,
        ),
        compiler_params=pltpu.CompilerParams(vmem_limit_bytes=grant << 20),
    )(*lens, *args)


def on_device(queries, keys_values, out_grads, doc_lengths):
    kv, q, dout = keys_values[0], queries[0], out_grads[0]
    rows, wide = kv.shape
    keys = (REACH + 1) * rows
    array = jax.ShapeDtypeStruct
    block = array((rows, wide), BF16)
    square = array((rows, HQ * rows), F32)
    stat = array((8, HQ * rows), F32)

    def exponentials(block_kv, offset_of):
        return call(
            functools.partial(block_kernel, offset_of), (), (docs, q, dout, block_kv),
            [stat, square, square],
            [pltpu.VMEM((rows, rows), F32), pltpu.VMEM((SLOTS, rows, 2 * rows), F32)],
            2 * rows, 4,
        )

    near = one_three(kv)
    far = three_one(kv)
    lens = all_lengths(doc_lengths)
    (causal,) = call(causal_kernel, (), (), [array((rows, rows), F32)], [], 100 * keys, 1)
    s_own, dp_own = call(products_kernel, (), (q, dout, kv), [square, square], [], 2 * rows, 4)
    own_stats, p_own, docs = call(
        own_kernel, lens, (s_own, dp_own, causal),
        [stat, square, array((8, rows), jnp.int32)], [pltpu.VMEM((rows, rows), F32)],
        rows, 2,
    )
    side = swapped(near)
    near_stats, p_near, dp_near = exponentials(near, lambda: 1 + 2 * is_odd())
    side_stats, p_side, dp_side = exponentials(side, lambda: 2)
    final, ds_far, g_far = call(
        far_kernel, (),
        (docs, q, dout, far, own_stats, near_stats, side_stats),
        [stat, array((rows, HQ * rows), BF16), block],
        [pltpu.VMEM((rows, rows), F32)]
        + [pltpu.VMEM((SLOTS, rows, 2 * rows), F32)] * 3
        + [pltpu.VMEM((SLOTS, 8, 2 * rows), F32)]
        + [pltpu.VMEM((2, rows, GROUP * rows), BF16)],
        4 * rows, 6,
    )
    relayed = moved(g_far, lambda i: -1 if i % 2 else i - 2)
    g_near, g_pair, ds_mid = call(
        mid_kernel, (),
        (q, dout, p_near, dp_near, p_side, dp_side, final, g_far),
        [
            block,
            array((2 * rows, wide), BF16),
            array((2 * rows, HQ * rows), BF16),
        ],
        [pltpu.VMEM((2, 2 * rows, GROUP * rows), BF16)], 4 * rows, 4,
    )
    pair_back = swapped(g_pair)
    (odd_sum,) = call(sum_kernel, (), (g_near, pair_back), [block], [], 1, 1)
    odd_back = moved(odd_sum, lambda i: i - 3 if i % 2 else -1)
    (joined,) = call(sum_kernel, (), (g_near, pair_back, relayed), [block], [], 1, 1)
    even_back = moved(joined, lambda i: -1 if i % 2 else i - 1)
    dq, own = call(
        query_kernel, (),
        (q, dout, kv, near, side, far, p_own, dp_own, final, ds_mid, ds_far),
        [array(q.shape, BF16), array((rows, wide), F32)],
        [pltpu.VMEM((HK, HD, keys), BF16)]
        + [pltpu.VMEM((2, rows, GROUP * rows), BF16)] * 2,
        2 * rows + keys, 6,
    )
    (total,) = call(finish_kernel, (), (own, pair_back, odd_back, even_back), [block], [], 1, 3)
    return (dq[None], total[None])


def solution(mesh):
    spec = P("pipe", "ctx", None)
    return jax.shard_map(
        on_device,
        mesh=mesh,
        in_specs=(spec, spec, spec, P("pipe")),
        out_specs=(spec, spec),
        check_vma=False,
    )
```

```python
import functools
import math

import jax
import jax.numpy as jnp
from jax import lax
from jax.experimental import pallas as pl
from jax.experimental.pallas import tpu as pltpu
from jax.sharding import PartitionSpec as P


HQ = 32
HK = 4
HD = 128
REACH = 3
GROUP = HQ // HK
F32 = jnp.float32
BF16 = jnp.bfloat16
NT = (((1,), (1,)), ((), ()))
NN = (((1,), (0,)), ((), ()))
SCALE = 1.0 / math.sqrt(HD)
RATE = SCALE * math.log2(math.e)
PAIRS = HQ // 2
PER_GROUP = GROUP // 2
SLOTS = 4


def moved(value, target_of):
    count = lax.axis_size("ctx")
    pairs = [(i, target_of(i)) for i in range(count)]
    return lax.ppermute(value, "ctx", [(s, t) for s, t in pairs if 0 <= t < count])


def one_three(value):
    return moved(value, lambda i: i + 1 if i % 2 else i + 3)


def three_one(value):
    return moved(value, lambda i: i + 3 if i % 2 else i + 1)


def swapped(value):
    return moved(value, lambda i: i ^ 1)


def all_lengths(lengths):
    count = lax.axis_size("pipe")
    pieces, stride = [lengths], 1
    while stride < count:
        pieces.append(
            lax.ppermute(jnp.concatenate(pieces), "pipe", [(i, i ^ stride) for i in range(count)])
        )
        stride *= 2
    return pieces


def positions(rows):
    return lax.axis_index("ctx") * rows + lax.broadcasted_iota(jnp.int32, (1, rows), 1)


def find_doc_starts(lens_refs, starts_scr, rows):
    pipe = lax.axis_index("pipe")
    t_pos = positions(rows)
    per_pipe = lens_refs[0].shape[0]
    place = 0
    for ref in lens_refs:
        for k in range(ref.shape[0]):
            starts_scr[((place // per_pipe) ^ pipe) * per_pipe + place % per_pipe] = ref[k]
            place += 1
    start, doc_start = jnp.int32(0), jnp.zeros((1, rows), jnp.int32)
    for d in range(place):
        doc_start = jnp.where(t_pos >= start, start, doc_start)
        start = start + starts_scr[d]
    return doc_start


def bias_of(doc_start, offset, base):
    rows = doc_start.shape[1]
    u_pos = (lax.axis_index("ctx") - offset) * rows
    u_pos = u_pos + lax.broadcasted_iota(jnp.int32, (rows, rows), 0)
    return jnp.where(u_pos >= doc_start, base, -1e30).astype(F32)


def reaches(docs_ref, offset):
    rows = docs_ref.shape[1]
    return docs_ref[0:1, 0:1][0, 0] < (lax.axis_index("ctx") - offset + 1) * rows


def is_odd():
    return lax.rem(lax.axis_index("ctx"), 2)


def at(i, width):
    return slice(i * width, (i + 1) * width)


def stacked(ref, first, count):
    return jnp.concatenate([ref[:, at(first + k, HD)] for k in range(count)], axis=0)


def scores_of(kv_ref, q_ref, i):
    return lax.dot_general(
        kv_ref[:, at(i // PER_GROUP, HD)], stacked(q_ref, 2 * i, 2), NT, preferred_element_type=F32
    )


def dweights_of(kv_ref, d_ref, i):
    return lax.dot_general(
        kv_ref[:, at(HK + i // PER_GROUP, HD)], stacked(d_ref, 2 * i, 2), NT,
        preferred_element_type=F32,
    )


def twice(value):
    return jnp.concatenate([value, value], axis=1)


def pipelined(stages):
    for step in range(PAIRS + len(stages) - 1):
        for k, stage in enumerate(stages):
            if 0 <= step - k < PAIRS:
                stage(step - k)


def at_group_end(action):
    def stage(i):
        if i % PER_GROUP == PER_GROUP - 1:
            action(i // PER_GROUP)

    return stage


def products_kernel(n_lens, q_ref, d_ref, kv_ref, s_ref, dp_ref):
    rows = q_ref.shape[0]
    for i in range(PAIRS):
        s_ref[:, at(i, 2 * rows)] = scores_of(kv_ref, q_ref, i)
        dp_ref[:, at(i, 2 * rows)] = dweights_of(kv_ref, d_ref, i)


def causal_kernel(n_lens, causal_ref):
    u = lax.broadcasted_iota(jnp.int32, causal_ref.shape, 0)
    t = lax.broadcasted_iota(jnp.int32, causal_ref.shape, 1)
    causal_ref[...] = jnp.where(u <= t, 0.0, -1e30).astype(F32)


def keep_exponentials(s, dp, column, stats_ref, p_ref):
    top = jnp.max(s, axis=0, keepdims=True)
    p = jnp.exp2((s - top) * RATE)
    p_ref[:, column] = p
    stats_ref[0:1, column] = top
    stats_ref[1:2, column] = jnp.sum(p, axis=0, keepdims=True)
    stats_ref[2:3, column] = jnp.sum(p * dp, axis=0, keepdims=True)


def own_kernel(n_lens, *refs):
    lens_refs, refs = refs[:n_lens], refs[n_lens:]
    s_ref, dp_ref, causal_ref, stats_ref, p_ref, docs_ref, starts_scr, bias_scr = refs
    rows = s_ref.shape[0]
    doc_start = find_doc_starts(lens_refs, starts_scr, rows)
    docs_ref[0:1] = doc_start
    bias_scr[...] = bias_of(doc_start, 0, causal_ref[...])
    for i in range(PAIRS):
        column = at(i, 2 * rows)
        s = s_ref[:, column] + twice(bias_scr[...])
        keep_exponentials(s, dp_ref[:, column], column, stats_ref, p_ref)


def block_kernel(offset_of, n_lens, *refs):
    docs_ref, q_ref, d_ref, kv_ref, stats_ref, p_ref, dp_ref, bias_scr, s_scr = refs
    rows = q_ref.shape[0]
    needed = reaches(docs_ref, offset_of())

    def first(i):
        s_scr[i % SLOTS] = scores_of(kv_ref, q_ref, i) + twice(bias_scr[...])
        dp_ref[:, at(i, 2 * rows)] = dweights_of(kv_ref, d_ref, i)

    def second(i):
        column = at(i, 2 * rows)
        keep_exponentials(s_scr[i % SLOTS], dp_ref[:, column], column, stats_ref, p_ref)

    @pl.when(needed)
    def _():
        bias_scr[...] = bias_of(docs_ref[0:1], offset_of(), 0.0)
        pipelined([first, second])

    @pl.when(jnp.logical_not(needed))
    def _():
        p_ref[...] = jnp.zeros_like(p_ref)
        dp_ref[...] = jnp.zeros_like(dp_ref)
        stats_ref[0:1] = jnp.full((1, stats_ref.shape[1]), -1e30, F32)
        stats_ref[1:3] = jnp.zeros((2, stats_ref.shape[1]), F32)


def far_kernel(n_lens, *refs):
    docs_ref, q_ref, d_ref, kv_ref = refs[:4]
    stats_refs = refs[4:7]
    final_ref, ds_ref, g_ref = refs[7:10]
    bias_scr, s_scr, dp_scr, p_scr, row_scr, w_scr = refs[10:]
    rows = q_ref.shape[0]
    offset = 3 - 2 * is_odd()
    needed = reaches(docs_ref, offset)

    def combined(top, column, total, dot):
        shares = [jnp.exp2((ref[0:1, column] - top) * RATE) for ref in stats_refs]
        for ref, share in zip(stats_refs, shares):
            total = total + ref[1:2, column] * share
            dot = dot + ref[2:3, column] * share
        inv = 1.0 / total
        delta = dot * inv
        final_ref[0:1, column] = delta
        for k, share in enumerate(shares):
            final_ref[k + 1:k + 2, column] = share * inv
        return inv, delta

    def first(i):
        s_scr[i % SLOTS] = scores_of(kv_ref, q_ref, i) + twice(bias_scr[...])
        dp_scr[i % SLOTS] = dweights_of(kv_ref, d_ref, i)

    def second(i):
        column = at(i, 2 * rows)
        s = s_scr[i % SLOTS]
        tops = [ref[0:1, column] for ref in stats_refs]
        top = functools.reduce(jnp.maximum, tops, jnp.max(s, axis=0, keepdims=True))
        p = jnp.exp2((s - top) * RATE)
        p_scr[i % SLOTS] = p
        total = jnp.sum(p, axis=0, keepdims=True)
        dot = jnp.sum(p * dp_scr[i % SLOTS], axis=0, keepdims=True)
        inv, delta = combined(top, column, total, dot)
        row_scr[i % SLOTS, 0:1] = inv
        row_scr[i % SLOTS, 1:2] = delta

    def third(i):
        w = p_scr[i % SLOTS] * row_scr[i % SLOTS, 0:1]
        ds = (w * (dp_scr[i % SLOTS] - row_scr[i % SLOTS, 1:2])).astype(BF16)
        ds_ref[:, at(i, 2 * rows)] = ds
        w_scr[i // PER_GROUP % 2, :, at(i % PER_GROUP, 2 * rows)] = w.astype(BF16)

    def gradients(group):
        dk = lax.dot_general(
            ds_ref[:, at(group, GROUP * rows)], stacked(q_ref, group * GROUP, GROUP), NN,
            preferred_element_type=F32,
        )
        g_ref[:, at(group, HD)] = (dk * SCALE).astype(BF16)
        dv = lax.dot_general(
            w_scr[group % 2], stacked(d_ref, group * GROUP, GROUP), NN, preferred_element_type=F32
        )
        g_ref[:, at(HK + group, HD)] = dv.astype(BF16)

    @pl.when(needed)
    def _():
        bias_scr[...] = bias_of(docs_ref[0:1], offset, 0.0)
        pipelined([first, second, third, at_group_end(gradients)])

    @pl.when(jnp.logical_not(needed))
    def _():
        g_ref[...] = jnp.zeros_like(g_ref)
        ds_ref[...] = jnp.zeros_like(ds_ref)
        column = slice(0, final_ref.shape[1])
        top = functools.reduce(jnp.maximum, [ref[0:1, column] for ref in stats_refs])
        zero = jnp.zeros_like(top)
        combined(top, column, zero, zero)


def mid_kernel(n_lens, *refs):
    docs_ref, q_ref, d_ref, p1_ref, dp1_ref, p2_ref, dp2_ref, final_ref, far_ref = refs[:9]
    near_ref, pair_ref, ds_ref, w_scr = refs[9:]
    rows = q_ref.shape[0]
    needed = reaches(docs_ref, 1 + is_odd())
    pair_ref[rows:] = far_ref[...]

    def first(i):
        column = at(i, 2 * rows)
        for b, (p_ref, dp_ref) in enumerate(((p1_ref, dp1_ref), (p2_ref, dp2_ref))):
            w = p_ref[:, column] * final_ref[b + 2:b + 3, column]
            ds = (w * (dp_ref[:, column] - final_ref[0:1, column])).astype(BF16)
            ds_ref[at(b, rows), column] = ds
            w_scr[i // PER_GROUP % 2, at(b, rows), at(i % PER_GROUP, 2 * rows)] = w.astype(BF16)

    def key_grads(group):
        dk = lax.dot_general(
            ds_ref[:, at(group, GROUP * rows)], stacked(q_ref, group * GROUP, GROUP), NN,
            preferred_element_type=F32,
        )
        dk = (dk * SCALE).astype(BF16)
        near_ref[:, at(group, HD)] = dk[:rows]
        pair_ref[:rows, at(group, HD)] = dk[rows:]

    def value_grads(group):
        dv = lax.dot_general(
            w_scr[group % 2], stacked(d_ref, group * GROUP, GROUP), NN, preferred_element_type=F32
        ).astype(BF16)
        near_ref[:, at(HK + group, HD)] = dv[:rows]
        pair_ref[:rows, at(HK + group, HD)] = dv[rows:]

    @pl.when(needed)
    def _():
        pipelined([first, at_group_end(key_grads), at_group_end(value_grads)])

    @pl.when(jnp.logical_not(needed))
    def _():
        near_ref[...] = jnp.zeros_like(near_ref)
        pair_ref[:rows] = jnp.zeros_like(near_ref)
        ds_ref[...] = jnp.zeros_like(ds_ref)


def sum_kernel(n_lens, near_ref, pair_ref, *refs):
    rows = near_ref.shape[0]
    total = near_ref[...].astype(F32) + pair_ref[:rows].astype(F32)
    for ref in refs[:-1]:
        total = total + ref[...].astype(F32)
    refs[-1][...] = total.astype(BF16)


def finish_kernel(n_lens, own_ref, pair_ref, odd_ref, even_ref, total_ref):
    rows = own_ref.shape[0]
    even = lax.rem(lax.axis_index("ctx"), 2) == 0
    chip = pair_ref[rows:].astype(F32) + odd_ref[...].astype(F32)
    moved_in = jnp.where(even, chip, even_ref[...].astype(F32))
    total_ref[...] = (own_ref[...] + moved_in).astype(BF16)


def query_kernel(n_lens, *refs):
    q_ref, d_ref, kv0_ref, kv1_ref, kv2_ref, kv3_ref = refs[:6]
    p_ref, dp_ref, final_ref, mid_ref, far_ref, dq_ref, own_ref, kt_scr, ds_scr, w_scr = refs[6:]
    rows = q_ref.shape[0]
    kv_refs = [kv0_ref, kv1_ref, kv2_ref, kv3_ref]

    def first(i):
        group = i // PER_GROUP
        if i % PER_GROUP == 0:
            for b, ref in enumerate(kv_refs):
                kt_scr[group, :, at(b, rows)] = ref[:, at(group, HD)].T
        column = at(i, 2 * rows)
        half, part = group % 2, at(i % PER_GROUP, 2 * rows)
        w = p_ref[:, column] * final_ref[1:2, column]
        ds_scr[half, :, part] = (w * (dp_ref[:, column] - final_ref[0:1, column])).astype(BF16)
        w_scr[half, :, part] = w.astype(BF16)

    def second(i):
        half, part = i // PER_GROUP % 2, at(i % PER_GROUP, 2 * rows)
        column = at(i, 2 * rows)
        ds = jnp.concatenate(
            [ds_scr[half, :, part], mid_ref[:, column], far_ref[:, column]], axis=0
        )
        dqt = lax.dot_general(kt_scr[i // PER_GROUP], ds, NN, preferred_element_type=F32)
        dq = (dqt * SCALE).astype(BF16).T
        dq_ref[:, at(2 * i, HD)] = dq[:rows]
        dq_ref[:, at(2 * i + 1, HD)] = dq[rows:]

    def own_grads(group):
        own_ref[:, at(group, HD)] = SCALE * lax.dot_general(
            ds_scr[group % 2], stacked(q_ref, group * GROUP, GROUP), NN, preferred_element_type=F32
        )
        own_ref[:, at(HK + group, HD)] = lax.dot_general(
            w_scr[group % 2], stacked(d_ref, group * GROUP, GROUP), NN, preferred_element_type=F32
        )

    pipelined([first, second, at_group_end(own_grads)])


def call(body, lens, args, outs, scratch, matmul_rows, grant):
    specs = [pl.BlockSpec(memory_space=pltpu.SMEM)] * len(lens)
    specs += [pl.BlockSpec(memory_space=pltpu.VMEM)] * len(args)
    docs = sum(x.shape[0] for x in lens)
    return pl.pallas_call(
        functools.partial(body, len(lens)),
        in_specs=specs,
        out_specs=[pl.BlockSpec(memory_space=pltpu.VMEM)] * len(outs),
        out_shape=outs,
        scratch_shapes=([pltpu.SMEM((docs,), jnp.int32)] if lens else []) + scratch,
        cost_estimate=pl.CostEstimate(
            flops=2 * HQ * HD * HD * matmul_rows,
            bytes_accessed=sum(x.size * x.dtype.itemsize for x in list(args) + list(outs)),
            transcendentals=0,
        ),
        compiler_params=pltpu.CompilerParams(vmem_limit_bytes=grant << 20),
    )(*lens, *args)


def on_device(queries, keys_values, out_grads, doc_lengths):
    kv, q, dout = keys_values[0], queries[0], out_grads[0]
    rows, wide = kv.shape
    keys = (REACH + 1) * rows
    array = jax.ShapeDtypeStruct
    block = array((rows, wide), BF16)
    square = array((rows, HQ * rows), F32)
    stat = array((8, HQ * rows), F32)

    def exponentials(block_kv, offset_of):
        return call(
            functools.partial(block_kernel, offset_of), (), (docs, q, dout, block_kv),
            [stat, square, square],
            [pltpu.VMEM((rows, rows), F32), pltpu.VMEM((SLOTS, rows, 2 * rows), F32)],
            2 * rows, 4,
        )

    near = one_three(kv)
    far = three_one(kv)
    lens = all_lengths(doc_lengths)
    (causal,) = call(causal_kernel, (), (), [array((rows, rows), F32)], [], 100 * keys, 1)
    s_own, dp_own = call(products_kernel, (), (q, dout, kv), [square, square], [], 2 * rows, 4)
    own_stats, p_own, docs = call(
        own_kernel, lens, (s_own, dp_own, causal),
        [stat, square, array((8, rows), jnp.int32)], [pltpu.VMEM((rows, rows), F32)],
        rows, 2,
    )
    side = swapped(near)
    near_stats, p_near, dp_near = exponentials(near, lambda: 1 + 2 * is_odd())
    side_stats, p_side, dp_side = exponentials(side, lambda: 2)
    final, ds_far, g_far = call(
        far_kernel, (),
        (docs, q, dout, far, own_stats, near_stats, side_stats),
        [stat, array((rows, HQ * rows), BF16), block],
        [pltpu.VMEM((rows, rows), F32)]
        + [pltpu.VMEM((SLOTS, rows, 2 * rows), F32)] * 3
        + [pltpu.VMEM((SLOTS, 8, 2 * rows), F32)]
        + [pltpu.VMEM((2, rows, GROUP * rows), BF16)],
        4 * rows, 6,
    )
    relayed = moved(g_far, lambda i: -1 if i % 2 or i < REACH else i - 2)
    g_near, g_pair, ds_mid = call(
        mid_kernel, (),
        (docs, q, dout, p_near, dp_near, p_side, dp_side, final, g_far),
        [
            block,
            array((2 * rows, wide), BF16),
            array((2 * rows, HQ * rows), BF16),
        ],
        [pltpu.VMEM((2, 2 * rows, GROUP * rows), BF16)], 4 * rows, 4,
    )
    pair_back = swapped(g_pair)
    (odd_sum,) = call(sum_kernel, (), (g_near, pair_back), [block], [], 1, 1)
    odd_back = moved(odd_sum, lambda i: i - 3 if i % 2 else -1)
    (joined,) = call(sum_kernel, (), (g_near, pair_back, relayed), [block], [], 1, 1)
    even_back = moved(joined, lambda i: -1 if i % 2 else i - 1)
    dq, own = call(
        query_kernel, (),
        (q, dout, kv, near, side, far, p_own, dp_own, final, ds_mid, ds_far),
        [array(q.shape, BF16), array((rows, wide), F32)],
        [pltpu.VMEM((HK, HD, keys), BF16)]
        + [pltpu.VMEM((2, rows, GROUP * rows), BF16)] * 2,
        2 * rows + keys, 6,
    )
    (total,) = call(finish_kernel, (), (own, pair_back, odd_back, even_back), [block], [], 1, 3)
    return (dq[None], total[None])


def solution(mesh):
    spec = P("pipe", "ctx", None)
    return jax.shard_map(
        on_device,
        mesh=mesh,
        in_specs=(spec, spec, spec, P("pipe")),
        out_specs=(spec, spec),
        check_vma=False,
    )
```

```python
import functools
import math

import jax
import jax.numpy as jnp
from jax import lax
from jax.experimental import pallas as pl
from jax.experimental.pallas import tpu as pltpu
from jax.sharding import PartitionSpec as P


HQ = 32
HK = 4
HD = 128
REACH = 3
GROUP = HQ // HK
F32 = jnp.float32
BF16 = jnp.bfloat16
NT = (((1,), (1,)), ((), ()))
NN = (((1,), (0,)), ((), ()))
SCALE = 1.0 / math.sqrt(HD)
RATE = SCALE * math.log2(math.e)
PAIRS = HQ // 2
PER_GROUP = GROUP // 2
SLOTS = 4


def moved(value, target_of):
    count = lax.axis_size("ctx")
    pairs = [(i, target_of(i)) for i in range(count)]
    return lax.ppermute(value, "ctx", [(s, t) for s, t in pairs if 0 <= t < count])


def one_three(value):
    return moved(value, lambda i: i + 1 if i % 2 else i + 3)


def swapped(value):
    return moved(value, lambda i: i ^ 1)


def all_lengths(lengths):
    count = lax.axis_size("pipe")
    pieces, stride = [lengths], 1
    while stride < count:
        pieces.append(
            lax.ppermute(jnp.concatenate(pieces), "pipe", [(i, i ^ stride) for i in range(count)])
        )
        stride *= 2
    return pieces


def positions(rows):
    return lax.axis_index("ctx") * rows + lax.broadcasted_iota(jnp.int32, (1, rows), 1)


def find_doc_starts(lens_refs, starts_scr, rows):
    pipe = lax.axis_index("pipe")
    t_pos = positions(rows)
    per_pipe = lens_refs[0].shape[0]
    place = 0
    for ref in lens_refs:
        for k in range(ref.shape[0]):
            starts_scr[((place // per_pipe) ^ pipe) * per_pipe + place % per_pipe] = ref[k]
            place += 1
    start, doc_start = jnp.int32(0), jnp.zeros((1, rows), jnp.int32)
    for d in range(place):
        doc_start = jnp.where(t_pos >= start, start, doc_start)
        start = start + starts_scr[d]
    return doc_start


def bias_of(doc_start, offset, base):
    rows = doc_start.shape[1]
    u_pos = (lax.axis_index("ctx") - offset) * rows
    u_pos = u_pos + lax.broadcasted_iota(jnp.int32, (rows, rows), 0)
    return jnp.where(u_pos >= doc_start, base, -1e30).astype(F32)


def reaches(docs_ref, offset):
    rows = docs_ref.shape[1]
    return docs_ref[0:1, 0:1][0, 0] < (lax.axis_index("ctx") - offset + 1) * rows


def is_odd():
    return lax.rem(lax.axis_index("ctx"), 2)


def at(i, width):
    return slice(i * width, (i + 1) * width)


def stacked(ref, first, count):
    return jnp.concatenate([ref[:, at(first + k, HD)] for k in range(count)], axis=0)


def scores_of(kv_ref, q_ref, i):
    return lax.dot_general(
        kv_ref[:, at(i // PER_GROUP, HD)], stacked(q_ref, 2 * i, 2), NT, preferred_element_type=F32
    )


def dweights_of(kv_ref, d_ref, i):
    return lax.dot_general(
        kv_ref[:, at(HK + i // PER_GROUP, HD)], stacked(d_ref, 2 * i, 2), NT,
        preferred_element_type=F32,
    )


def twice(value):
    return jnp.concatenate([value, value], axis=1)


def pipelined(stages):
    for step in range(PAIRS + len(stages) - 1):
        for k, stage in enumerate(stages):
            if 0 <= step - k < PAIRS:
                stage(step - k)


def at_group_end(action):
    def stage(i):
        if i % PER_GROUP == PER_GROUP - 1:
            action(i // PER_GROUP)

    return stage


def products_kernel(n_lens, q_ref, d_ref, kv_ref, s_ref, dp_ref):
    rows = q_ref.shape[0]
    for i in range(PAIRS):
        s_ref[:, at(i, 2 * rows)] = scores_of(kv_ref, q_ref, i)
        dp_ref[:, at(i, 2 * rows)] = dweights_of(kv_ref, d_ref, i)


def causal_kernel(n_lens, causal_ref):
    u = lax.broadcasted_iota(jnp.int32, causal_ref.shape, 0)
    t = lax.broadcasted_iota(jnp.int32, causal_ref.shape, 1)
    causal_ref[...] = jnp.where(u <= t, 0.0, -1e30).astype(F32)


def keep_exponentials(s, dp, column, stats_ref, p_ref):
    top = jnp.max(s, axis=0, keepdims=True)
    p = jnp.exp2((s - top) * RATE)
    p_ref[:, column] = p
    stats_ref[0:1, column] = top
    stats_ref[1:2, column] = jnp.sum(p, axis=0, keepdims=True)
    stats_ref[2:3, column] = jnp.sum(p * dp, axis=0, keepdims=True)


def own_kernel(n_lens, *refs):
    lens_refs, refs = refs[:n_lens], refs[n_lens:]
    s_ref, dp_ref, causal_ref, stats_ref, p_ref, docs_ref, starts_scr, bias_scr = refs
    rows = s_ref.shape[0]
    doc_start = find_doc_starts(lens_refs, starts_scr, rows)
    docs_ref[0:1] = doc_start
    bias_scr[...] = bias_of(doc_start, 0, causal_ref[...])
    for i in range(PAIRS):
        column = at(i, 2 * rows)
        s = s_ref[:, column] + twice(bias_scr[...])
        keep_exponentials(s, dp_ref[:, column], column, stats_ref, p_ref)


def pick(even_ref, odd_ref, picked_ref, width):
    odd = is_odd()

    @pl.when(odd == 0)
    def _():
        picked_ref[...] = even_ref[:, :width]

    @pl.when(odd == 1)
    def _():
        picked_ref[...] = odd_ref[:, :width]


def block_kernel(offset, n_lens, *refs):
    docs_ref, q_ref, d_ref, even_ref, odd_ref, stats_ref, p_ref, dp_ref = refs[:8]
    bias_scr, s_scr, kv_scr = refs[8:]
    rows = q_ref.shape[0]
    needed = reaches(docs_ref, offset)
    kv_ref = kv_scr if offset == 1 else even_ref

    def first(i):
        s_scr[i % SLOTS] = scores_of(kv_ref, q_ref, i) + twice(bias_scr[...])
        dp_ref[:, at(i, 2 * rows)] = dweights_of(kv_ref, d_ref, i)

    def second(i):
        column = at(i, 2 * rows)
        keep_exponentials(s_scr[i % SLOTS], dp_ref[:, column], column, stats_ref, p_ref)

    @pl.when(needed)
    def _():
        if offset == 1:
            pick(even_ref, odd_ref, kv_scr, kv_scr.shape[1])
        bias_scr[...] = bias_of(docs_ref[0:1], offset, 0.0)
        pipelined([first, second])

    @pl.when(jnp.logical_not(needed))
    def _():
        p_ref[...] = jnp.zeros_like(p_ref)
        dp_ref[...] = jnp.zeros_like(dp_ref)
        stats_ref[0:1] = jnp.full((1, stats_ref.shape[1]), -1e30, F32)
        stats_ref[1:3] = jnp.zeros((2, stats_ref.shape[1]), F32)


def far_kernel(n_lens, *refs):
    docs_ref, q_ref, d_ref, even_ref, odd_ref = refs[:5]
    stats_refs = refs[5:8]
    final_ref, ds_ref, g_ref = refs[8:11]
    bias_scr, s_scr, dp_scr, p_scr, row_scr, w_scr, kv_ref = refs[11:]
    rows = q_ref.shape[0]
    needed = reaches(docs_ref, REACH)

    def combined(top, column, total, dot):
        shares = [jnp.exp2((ref[0:1, column] - top) * RATE) for ref in stats_refs]
        for ref, share in zip(stats_refs, shares):
            total = total + ref[1:2, column] * share
            dot = dot + ref[2:3, column] * share
        inv = 1.0 / total
        delta = dot * inv
        final_ref[0:1, column] = delta
        for k, share in enumerate(shares):
            final_ref[k + 1:k + 2, column] = share * inv
        return inv, delta

    def first(i):
        s_scr[i % SLOTS] = scores_of(kv_ref, q_ref, i) + twice(bias_scr[...])
        dp_scr[i % SLOTS] = dweights_of(kv_ref, d_ref, i)

    def second(i):
        column = at(i, 2 * rows)
        s = s_scr[i % SLOTS]
        tops = [ref[0:1, column] for ref in stats_refs]
        top = functools.reduce(jnp.maximum, tops, jnp.max(s, axis=0, keepdims=True))
        p = jnp.exp2((s - top) * RATE)
        p_scr[i % SLOTS] = p
        total = jnp.sum(p, axis=0, keepdims=True)
        dot = jnp.sum(p * dp_scr[i % SLOTS], axis=0, keepdims=True)
        inv, delta = combined(top, column, total, dot)
        row_scr[i % SLOTS, 0:1] = inv
        row_scr[i % SLOTS, 1:2] = delta

    def third(i):
        w = p_scr[i % SLOTS] * row_scr[i % SLOTS, 0:1]
        ds = (w * (dp_scr[i % SLOTS] - row_scr[i % SLOTS, 1:2])).astype(BF16)
        ds_ref[:, at(i, 2 * rows)] = ds
        w_scr[i // PER_GROUP % 2, :, at(i % PER_GROUP, 2 * rows)] = w.astype(BF16)

    def gradients(group):
        dk = lax.dot_general(
            ds_ref[:, at(group, GROUP * rows)], stacked(q_ref, group * GROUP, GROUP), NN,
            preferred_element_type=F32,
        )
        g_ref[:, at(group, HD)] = (dk * SCALE).astype(BF16)
        dv = lax.dot_general(
            w_scr[group % 2], stacked(d_ref, group * GROUP, GROUP), NN, preferred_element_type=F32
        )
        g_ref[:, at(HK + group, HD)] = dv.astype(BF16)

    @pl.when(needed)
    def _():
        pick(even_ref, odd_ref, kv_ref, kv_ref.shape[1])
        bias_scr[...] = bias_of(docs_ref[0:1], REACH, 0.0)
        pipelined([first, second, third, at_group_end(gradients)])

    @pl.when(jnp.logical_not(needed))
    def _():
        g_ref[...] = jnp.zeros_like(g_ref)
        ds_ref[...] = jnp.zeros_like(ds_ref)
        column = slice(0, final_ref.shape[1])
        top = functools.reduce(jnp.maximum, [ref[0:1, column] for ref in stats_refs])
        zero = jnp.zeros_like(top)
        combined(top, column, zero, zero)


def mid_kernel(n_lens, *refs):
    docs_ref, q_ref, d_ref, p1_ref, dp1_ref, p2_ref, dp2_ref, final_ref = refs[:8]
    near_ref, pair_ref, ds_ref, w_scr = refs[8:]
    rows = q_ref.shape[0]
    terms = ((p1_ref, dp1_ref), (p2_ref, dp2_ref))

    def gradients_of(count):
        part = slice(0, count * rows)

        def first(i):
            column = at(i, 2 * rows)
            for b, (p_ref, dp_ref) in enumerate(terms[:count]):
                w = p_ref[:, column] * final_ref[b + 2:b + 3, column]
                ds = (w * (dp_ref[:, column] - final_ref[0:1, column])).astype(BF16)
                ds_ref[at(b, rows), column] = ds
                w_scr[i // PER_GROUP % 2, at(b, rows), at(i % PER_GROUP, 2 * rows)] = w.astype(BF16)

        def write(columns, value):
            near_ref[:, columns] = value[:rows]
            pair_ref[rows:, columns] = value[:rows]
            if count == 2:
                pair_ref[:rows, columns] = value[rows:]

        def key_grads(group):
            dk = lax.dot_general(
                ds_ref[part, at(group, GROUP * rows)], stacked(q_ref, group * GROUP, GROUP), NN,
                preferred_element_type=F32,
            )
            write(at(group, HD), (dk * SCALE).astype(BF16))

        def value_grads(group):
            dv = lax.dot_general(
                w_scr[group % 2, part], stacked(d_ref, group * GROUP, GROUP), NN,
                preferred_element_type=F32,
            )
            write(at(HK + group, HD), dv.astype(BF16))

        pipelined([first, at_group_end(key_grads), at_group_end(value_grads)])

    near_needed, side_needed = reaches(docs_ref, 1), reaches(docs_ref, 2)

    @pl.when(side_needed)
    def _():
        gradients_of(2)

    @pl.when(jnp.logical_not(side_needed))
    def _():
        ds_ref[rows:] = jnp.zeros_like(ds_ref[rows:])
        pair_ref[:rows] = jnp.zeros_like(near_ref)

    @pl.when(jnp.logical_and(near_needed, jnp.logical_not(side_needed)))
    def _():
        gradients_of(1)

    @pl.when(jnp.logical_not(near_needed))
    def _():
        ds_ref[:rows] = jnp.zeros_like(ds_ref[:rows])
        near_ref[...] = jnp.zeros_like(near_ref)
        pair_ref[rows:] = jnp.zeros_like(near_ref)


def odd_sum_kernel(n_lens, far_ref, pair_ref, sum_ref):
    rows = far_ref.shape[0]
    sum_ref[...] = (far_ref[...].astype(F32) + pair_ref[:rows].astype(F32)).astype(BF16)


def even_sum_kernel(n_lens, near_ref, pair_ref, relayed_ref, sum_ref):
    rows = near_ref.shape[0]
    total = near_ref[...].astype(F32) + pair_ref[:rows].astype(F32)
    sum_ref[...] = (total + relayed_ref[...].astype(F32)).astype(BF16)


def finish_kernel(n_lens, own_ref, pair_ref, odd_ref, even_ref, total_ref):
    rows = own_ref.shape[0]
    even = lax.rem(lax.axis_index("ctx"), 2) == 0
    chip = pair_ref[rows:].astype(F32) + odd_ref[...].astype(F32)
    moved_in = jnp.where(even, chip, even_ref[...].astype(F32))
    total_ref[...] = (own_ref[...] + moved_in).astype(BF16)


def query_kernel(n_lens, *refs):
    q_ref, d_ref, kv_ref, across_ref, chip_ref, side_ref, far_ref = refs[:7]
    p_ref, dp_ref, final_ref, mid_ref, ds_far_ref, dq_ref, own_ref = refs[7:14]
    kt_scr, ds_scr, w_scr, near_scr, far_scr = refs[14:]
    rows = q_ref.shape[0]
    pick(across_ref, chip_ref, near_scr, near_scr.shape[1])
    pick(far_ref, across_ref, far_scr, far_scr.shape[1])
    kv_refs = [kv_ref, near_scr, side_ref, far_scr]

    def first(i):
        group = i // PER_GROUP
        if i % PER_GROUP == 0:
            for b, ref in enumerate(kv_refs):
                kt_scr[group, :, at(b, rows)] = ref[:, at(group, HD)].T
        column = at(i, 2 * rows)
        half, part = group % 2, at(i % PER_GROUP, 2 * rows)
        w = p_ref[:, column] * final_ref[1:2, column]
        ds_scr[half, :, part] = (w * (dp_ref[:, column] - final_ref[0:1, column])).astype(BF16)
        w_scr[half, :, part] = w.astype(BF16)

    def second(i):
        half, part = i // PER_GROUP % 2, at(i % PER_GROUP, 2 * rows)
        column = at(i, 2 * rows)
        ds = jnp.concatenate(
            [ds_scr[half, :, part], mid_ref[:, column], ds_far_ref[:, column]], axis=0
        )
        dqt = lax.dot_general(kt_scr[i // PER_GROUP], ds, NN, preferred_element_type=F32)
        dq = (dqt * SCALE).astype(BF16).T
        dq_ref[:, at(2 * i, HD)] = dq[:rows]
        dq_ref[:, at(2 * i + 1, HD)] = dq[rows:]

    def own_grads(group):
        own_ref[:, at(group, HD)] = SCALE * lax.dot_general(
            ds_scr[group % 2], stacked(q_ref, group * GROUP, GROUP), NN, preferred_element_type=F32
        )
        own_ref[:, at(HK + group, HD)] = lax.dot_general(
            w_scr[group % 2], stacked(d_ref, group * GROUP, GROUP), NN, preferred_element_type=F32
        )

    pipelined([first, second, at_group_end(own_grads)])


def call(body, lens, args, outs, scratch, matmul_rows, grant):
    specs = [pl.BlockSpec(memory_space=pltpu.SMEM)] * len(lens)
    specs += [pl.BlockSpec(memory_space=pltpu.VMEM)] * len(args)
    docs = sum(x.shape[0] for x in lens)
    return pl.pallas_call(
        functools.partial(body, len(lens)),
        in_specs=specs,
        out_specs=[pl.BlockSpec(memory_space=pltpu.VMEM)] * len(outs),
        out_shape=outs,
        scratch_shapes=([pltpu.SMEM((docs,), jnp.int32)] if lens else []) + scratch,
        cost_estimate=pl.CostEstimate(
            flops=2 * HQ * HD * HD * matmul_rows,
            bytes_accessed=sum(x.size * x.dtype.itemsize for x in list(args) + list(outs)),
            transcendentals=0,
        ),
        compiler_params=pltpu.CompilerParams(vmem_limit_bytes=grant << 20),
    )(*lens, *args)


def on_device(queries, keys_values, out_grads, doc_lengths):
    kv, q, dout = keys_values[0], queries[0], out_grads[0]
    rows, wide = kv.shape
    keys = (REACH + 1) * rows
    array = jax.ShapeDtypeStruct
    block = array((rows, wide), BF16)
    square = array((rows, HQ * rows), F32)
    stat = array((8, HQ * rows), F32)

    def exponentials(even_kv, odd_kv, offset):
        return call(
            functools.partial(block_kernel, offset), (),
            (docs, q, dout, even_kv, odd_kv), [stat, square, square],
            [
                pltpu.VMEM((rows, rows), F32),
                pltpu.VMEM((SLOTS, rows, 2 * rows), F32),
                pltpu.VMEM((rows, wide), BF16),
            ],
            2 * rows, 4,
        )

    across = one_three(kv)
    far = moved(kv, lambda i: i + 3 if i % 2 else -1)
    chip = swapped(kv)
    lens = all_lengths(doc_lengths)
    (causal,) = call(causal_kernel, (), (), [array((rows, rows), F32)], [], 100 * keys, 1)
    s_own, dp_own = call(products_kernel, (), (q, dout, kv), [square, square], [], 2 * rows, 4)
    own_stats, p_own, docs = call(
        own_kernel, lens, (s_own, dp_own, causal),
        [stat, square, array((8, rows), jnp.int32)], [pltpu.VMEM((rows, rows), F32)],
        rows, 2,
    )
    side = swapped(across)
    near_stats, p_near, dp_near = exponentials(across, chip, 1)
    side_stats, p_side, dp_side = exponentials(side, side, 2)
    final, ds_far, g_far = call(
        far_kernel, (),
        (docs, q, dout, far, across, own_stats, near_stats, side_stats),
        [stat, array((rows, HQ * rows), BF16), block],
        [pltpu.VMEM((rows, rows), F32)]
        + [pltpu.VMEM((SLOTS, rows, 2 * rows), F32)] * 3
        + [pltpu.VMEM((SLOTS, 8, 2 * rows), F32)]
        + [pltpu.VMEM((2, rows, GROUP * rows), BF16), pltpu.VMEM((rows, wide), BF16)],
        4 * rows, 6,
    )
    relayed = moved(g_far, lambda i: -1 if i % 2 or i < REACH else i - 2)
    g_near, g_pair, ds_mid = call(
        mid_kernel, (),
        (docs, q, dout, p_near, dp_near, p_side, dp_side, final),
        [
            block,
            array((2 * rows, wide), BF16),
            array((2 * rows, HQ * rows), BF16),
        ],
        [pltpu.VMEM((2, 2 * rows, GROUP * rows), BF16)], 4 * rows, 4,
    )
    pair_back = swapped(g_pair)
    (odd_sum,) = call(odd_sum_kernel, (), (g_far, pair_back), [block], [], 1, 1)
    odd_back = moved(odd_sum, lambda i: i - 3 if i % 2 else -1)
    (joined,) = call(even_sum_kernel, (), (g_near, pair_back, relayed), [block], [], 1, 1)
    even_back = moved(joined, lambda i: -1 if i % 2 else i - 1)
    dq, own = call(
        query_kernel, (),
        (q, dout, kv, across, chip, side, far, p_own, dp_own, final, ds_mid, ds_far),
        [array(q.shape, BF16), array((rows, wide), F32)],
        [pltpu.VMEM((HK, HD, keys), BF16)]
        + [pltpu.VMEM((2, rows, GROUP * rows), BF16)] * 2
        + [pltpu.VMEM((rows, HK * HD), BF16)] * 2,
        2 * rows + keys, 6,
    )
    (total,) = call(finish_kernel, (), (own, pair_back, odd_back, even_back), [block], [], 1, 3)
    return (dq[None], total[None])


def solution(mesh):
    spec = P("pipe", "ctx", None)
    return jax.shard_map(
        on_device,
        mesh=mesh,
        in_specs=(spec, spec, spec, P("pipe")),
        out_specs=(spec, spec),
        check_vma=False,
    )
```

```python
import functools
import math

import jax
import jax.numpy as jnp
from jax import lax
from jax.experimental import pallas as pl
from jax.experimental.pallas import tpu as pltpu
from jax.sharding import PartitionSpec as P


HQ = 32
HK = 4
HD = 128
REACH = 3
GROUP = HQ // HK
F32 = jnp.float32
BF16 = jnp.bfloat16
NT = (((1,), (1,)), ((), ()))
NN = (((1,), (0,)), ((), ()))
SCALE = 1.0 / math.sqrt(HD)
RATE = SCALE * math.log2(math.e)
PAIRS = HQ // 2
PER_GROUP = GROUP // 2
SLOTS = 4


def moved(value, target_of):
    count = lax.axis_size("ctx")
    pairs = [(i, target_of(i)) for i in range(count)]
    return lax.ppermute(value, "ctx", [(s, t) for s, t in pairs if 0 <= t < count])


def one_three(value):
    return moved(value, lambda i: i + 1 if i % 2 else i + 3)


def swapped(value):
    return moved(value, lambda i: i ^ 1)


def all_lengths(lengths):
    count = lax.axis_size("pipe")
    pieces, stride = [lengths], 1
    while stride < count:
        pieces.append(
            lax.ppermute(jnp.concatenate(pieces), "pipe", [(i, i ^ stride) for i in range(count)])
        )
        stride *= 2
    return pieces


def positions(rows):
    return lax.axis_index("ctx") * rows + lax.broadcasted_iota(jnp.int32, (1, rows), 1)


def find_doc_starts(lens_refs, starts_scr, rows):
    pipe = lax.axis_index("pipe")
    t_pos = positions(rows)
    per_pipe = lens_refs[0].shape[0]
    place = 0
    for ref in lens_refs:
        for k in range(ref.shape[0]):
            starts_scr[((place // per_pipe) ^ pipe) * per_pipe + place % per_pipe] = ref[k]
            place += 1
    start, doc_start = jnp.int32(0), jnp.zeros((1, rows), jnp.int32)
    for d in range(place):
        doc_start = jnp.where(t_pos >= start, start, doc_start)
        start = start + starts_scr[d]
    return doc_start


def bias_of(doc_start, offset, base):
    rows = doc_start.shape[1]
    u_pos = (lax.axis_index("ctx") - offset) * rows
    u_pos = u_pos + lax.broadcasted_iota(jnp.int32, (rows, rows), 0)
    return jnp.where(u_pos >= doc_start, base, -1e30).astype(F32)


def reaches(docs_ref, offset):
    rows = docs_ref.shape[1]
    return docs_ref[0:1, 0:1][0, 0] < (lax.axis_index("ctx") - offset + 1) * rows


def is_odd():
    return lax.rem(lax.axis_index("ctx"), 2)


def at(i, width):
    return slice(i * width, (i + 1) * width)


def stacked(ref, first, count):
    return jnp.concatenate([ref[:, at(first + k, HD)] for k in range(count)], axis=0)


def scores_of(kv_ref, q_ref, i):
    return lax.dot_general(
        kv_ref[:, at(i // PER_GROUP, HD)], stacked(q_ref, 2 * i, 2), NT, preferred_element_type=F32
    )


def dweights_of(kv_ref, d_ref, i):
    return lax.dot_general(
        kv_ref[:, at(HK + i // PER_GROUP, HD)], stacked(d_ref, 2 * i, 2), NT,
        preferred_element_type=F32,
    )


def twice(value):
    return jnp.concatenate([value, value], axis=1)


def pipelined(stages):
    for step in range(PAIRS + len(stages) - 1):
        for k, stage in enumerate(stages):
            if 0 <= step - k < PAIRS:
                stage(step - k)


def at_group_end(action):
    def stage(i):
        if i % PER_GROUP == PER_GROUP - 1:
            action(i // PER_GROUP)

    return stage


def products_kernel(n_lens, q_ref, d_ref, kv_ref, s_ref, dp_ref):
    rows = q_ref.shape[0]
    for i in range(PAIRS):
        s_ref[:, at(i, 2 * rows)] = scores_of(kv_ref, q_ref, i)
        dp_ref[:, at(i, 2 * rows)] = dweights_of(kv_ref, d_ref, i)


def causal_kernel(n_lens, causal_ref):
    u = lax.broadcasted_iota(jnp.int32, causal_ref.shape, 0)
    t = lax.broadcasted_iota(jnp.int32, causal_ref.shape, 1)
    causal_ref[...] = jnp.where(u <= t, 0.0, -1e30).astype(F32)


def keep_exponentials(s, dp, column, stats_ref, p_ref):
    top = jnp.max(s, axis=0, keepdims=True)
    p = jnp.exp2((s - top) * RATE)
    p_ref[:, column] = p
    stats_ref[0:1, column] = top
    stats_ref[1:2, column] = jnp.sum(p, axis=0, keepdims=True)
    stats_ref[2:3, column] = jnp.sum(p * dp, axis=0, keepdims=True)


def own_kernel(n_lens, *refs):
    lens_refs, refs = refs[:n_lens], refs[n_lens:]
    s_ref, dp_ref, causal_ref, stats_ref, p_ref, docs_ref, starts_scr, bias_scr = refs
    rows = s_ref.shape[0]
    doc_start = find_doc_starts(lens_refs, starts_scr, rows)
    docs_ref[0:1] = doc_start
    bias_scr[...] = bias_of(doc_start, 0, causal_ref[...])
    for i in range(PAIRS):
        column = at(i, 2 * rows)
        s = s_ref[:, column] + twice(bias_scr[...])
        keep_exponentials(s, dp_ref[:, column], column, stats_ref, p_ref)


def pick(even_ref, odd_ref, picked_ref, width):
    picked_ref[...] = jnp.where(is_odd() == 1, odd_ref[:, :width], even_ref[:, :width])


def block_kernel(offset, n_lens, *refs):
    docs_ref, q_ref, d_ref, even_ref, odd_ref, stats_ref, p_ref, dp_ref = refs[:8]
    bias_scr, s_scr, kv_scr = refs[8:]
    rows = q_ref.shape[0]
    needed = reaches(docs_ref, offset)
    kv_ref = kv_scr if offset == 1 else even_ref

    def first(i):
        s_scr[i % SLOTS] = scores_of(kv_ref, q_ref, i) + twice(bias_scr[...])
        dp_ref[:, at(i, 2 * rows)] = dweights_of(kv_ref, d_ref, i)

    def second(i):
        column = at(i, 2 * rows)
        keep_exponentials(s_scr[i % SLOTS], dp_ref[:, column], column, stats_ref, p_ref)

    @pl.when(needed)
    def _():
        if offset == 1:
            pick(even_ref, odd_ref, kv_scr, kv_scr.shape[1])
        bias_scr[...] = bias_of(docs_ref[0:1], offset, 0.0)
        pipelined([first, second])

    @pl.when(jnp.logical_not(needed))
    def _():
        p_ref[...] = jnp.zeros_like(p_ref)
        dp_ref[...] = jnp.zeros_like(dp_ref)
        stats_ref[0:1] = jnp.full((1, stats_ref.shape[1]), -1e30, F32)
        stats_ref[1:3] = jnp.zeros((2, stats_ref.shape[1]), F32)


def far_kernel(n_lens, *refs):
    docs_ref, q_ref, d_ref, even_ref, odd_ref = refs[:5]
    stats_refs = refs[5:8]
    final_ref, ds_ref, g_ref = refs[8:11]
    bias_scr, s_scr, dp_scr, p_scr, row_scr, w_scr, kv_ref = refs[11:]
    rows = q_ref.shape[0]
    needed = reaches(docs_ref, REACH)

    def combined(top, column, total, dot):
        shares = [jnp.exp2((ref[0:1, column] - top) * RATE) for ref in stats_refs]
        for ref, share in zip(stats_refs, shares):
            total = total + ref[1:2, column] * share
            dot = dot + ref[2:3, column] * share
        inv = 1.0 / total
        delta = dot * inv
        final_ref[0:1, column] = delta
        for k, share in enumerate(shares):
            final_ref[k + 1:k + 2, column] = share * inv
        return inv, delta

    def run(skip):
        used, kept = slice(skip, rows), slice(0, rows - skip)
        kv_used = kv_ref.at[used]

        def first(i):
            s_scr[i % SLOTS, kept] = scores_of(kv_used, q_ref, i) + twice(bias_scr[used])
            dp_scr[i % SLOTS, kept] = dweights_of(kv_used, d_ref, i)

        def second(i):
            column = at(i, 2 * rows)
            s = s_scr[i % SLOTS, kept]
            tops = [ref[0:1, column] for ref in stats_refs]
            top = functools.reduce(jnp.maximum, tops, jnp.max(s, axis=0, keepdims=True))
            p = jnp.exp2((s - top) * RATE)
            p_scr[i % SLOTS, kept] = p
            total = jnp.sum(p, axis=0, keepdims=True)
            dot = jnp.sum(p * dp_scr[i % SLOTS, kept], axis=0, keepdims=True)
            inv, delta = combined(top, column, total, dot)
            row_scr[i % SLOTS, 0:1] = inv
            row_scr[i % SLOTS, 1:2] = delta

        def third(i):
            w = p_scr[i % SLOTS, kept] * row_scr[i % SLOTS, 0:1]
            ds = (w * (dp_scr[i % SLOTS, kept] - row_scr[i % SLOTS, 1:2])).astype(BF16)
            ds_ref[used, at(i, 2 * rows)] = ds
            w_scr[i // PER_GROUP % 2, kept, at(i % PER_GROUP, 2 * rows)] = w.astype(BF16)

        def gradients(group):
            dk = lax.dot_general(
                ds_ref[used, at(group, GROUP * rows)], stacked(q_ref, group * GROUP, GROUP), NN,
                preferred_element_type=F32,
            )
            g_ref[used, at(group, HD)] = (dk * SCALE).astype(BF16)
            dv = lax.dot_general(
                w_scr[group % 2, kept], stacked(d_ref, group * GROUP, GROUP), NN,
                preferred_element_type=F32,
            )
            g_ref[used, at(HK + group, HD)] = dv.astype(BF16)

        if skip:
            g_ref[:skip] = jnp.zeros((skip, g_ref.shape[1]), BF16)
            ds_ref[:skip] = jnp.zeros((skip, ds_ref.shape[1]), BF16)
        pick(even_ref, odd_ref, kv_ref, kv_ref.shape[1])
        bias_scr[...] = bias_of(docs_ref[0:1], REACH, 0.0)
        pipelined([first, second, third, at_group_end(gradients)])

    doc_start = docs_ref[0:1, 0:1][0, 0]
    middle = (lax.axis_index("ctx") - REACH) * rows + rows // 2

    @pl.when(jnp.logical_and(needed, doc_start < middle))
    def _():
        run(0)

    @pl.when(jnp.logical_and(needed, doc_start >= middle))
    def _():
        run(rows // 2)

    @pl.when(jnp.logical_not(needed))
    def _():
        g_ref[...] = jnp.zeros_like(g_ref)
        ds_ref[...] = jnp.zeros_like(ds_ref)
        column = slice(0, final_ref.shape[1])
        top = functools.reduce(jnp.maximum, [ref[0:1, column] for ref in stats_refs])
        zero = jnp.zeros_like(top)
        combined(top, column, zero, zero)


def mid_kernel(n_lens, *refs):
    docs_ref, q_ref, d_ref, p1_ref, dp1_ref, p2_ref, dp2_ref, final_ref = refs[:8]
    near_ref, pair_ref, ds_ref, w_scr = refs[8:]
    rows = q_ref.shape[0]
    terms = ((p1_ref, dp1_ref), (p2_ref, dp2_ref))

    def gradients_of(count):
        part = slice(0, count * rows)

        def first(i):
            column = at(i, 2 * rows)
            for b, (p_ref, dp_ref) in enumerate(terms[:count]):
                w = p_ref[:, column] * final_ref[b + 2:b + 3, column]
                ds = (w * (dp_ref[:, column] - final_ref[0:1, column])).astype(BF16)
                ds_ref[at(b, rows), column] = ds
                w_scr[i // PER_GROUP % 2, at(b, rows), at(i % PER_GROUP, 2 * rows)] = w.astype(BF16)

        def write(columns, value):
            near_ref[:, columns] = value[:rows]
            pair_ref[rows:, columns] = value[:rows]
            if count == 2:
                pair_ref[:rows, columns] = value[rows:]

        def key_grads(group):
            dk = lax.dot_general(
                ds_ref[part, at(group, GROUP * rows)], stacked(q_ref, group * GROUP, GROUP), NN,
                preferred_element_type=F32,
            )
            write(at(group, HD), (dk * SCALE).astype(BF16))

        def value_grads(group):
            dv = lax.dot_general(
                w_scr[group % 2, part], stacked(d_ref, group * GROUP, GROUP), NN,
                preferred_element_type=F32,
            )
            write(at(HK + group, HD), dv.astype(BF16))

        pipelined([first, at_group_end(key_grads), at_group_end(value_grads)])

    near_needed, side_needed = reaches(docs_ref, 1), reaches(docs_ref, 2)

    @pl.when(side_needed)
    def _():
        gradients_of(2)

    @pl.when(jnp.logical_not(side_needed))
    def _():
        ds_ref[rows:] = jnp.zeros_like(ds_ref[rows:])
        pair_ref[:rows] = jnp.zeros_like(near_ref)

    @pl.when(jnp.logical_and(near_needed, jnp.logical_not(side_needed)))
    def _():
        gradients_of(1)

    @pl.when(jnp.logical_not(near_needed))
    def _():
        ds_ref[:rows] = jnp.zeros_like(ds_ref[:rows])
        near_ref[...] = jnp.zeros_like(near_ref)
        pair_ref[rows:] = jnp.zeros_like(near_ref)


def odd_sum_kernel(n_lens, far_ref, pair_ref, sum_ref):
    rows = far_ref.shape[0]
    sum_ref[...] = (far_ref[...].astype(F32) + pair_ref[:rows].astype(F32)).astype(BF16)


def even_sum_kernel(n_lens, near_ref, pair_ref, relayed_ref, sum_ref):
    rows = near_ref.shape[0]
    total = near_ref[...].astype(F32) + pair_ref[:rows].astype(F32)
    sum_ref[...] = (total + relayed_ref[...].astype(F32)).astype(BF16)


def finish_kernel(n_lens, own_ref, pair_ref, odd_ref, even_ref, total_hbm, total_scr, sems):
    rows = own_ref.shape[0]
    even = lax.rem(lax.axis_index("ctx"), 2) == 0
    parts = sems.shape[0]
    step = rows // parts
    copies = []
    for k in range(parts):
        part = at(k, step)
        chip = pair_ref[rows + k * step:rows + (k + 1) * step].astype(F32)
        chip = chip + odd_ref[part].astype(F32)
        moved_in = jnp.where(even, chip, even_ref[part].astype(F32))
        total_scr[part] = (own_ref[part] + moved_in).astype(BF16)
        copies.append(pltpu.make_async_copy(total_scr.at[part], total_hbm.at[part], sems.at[k]))
        copies[k].start()
    for copy in copies:
        copy.wait()


def query_kernel(n_lens, *refs):
    q_ref, d_ref, kv_ref, across_ref, chip_ref, side_ref, far_ref = refs[:7]
    p_ref, dp_ref, final_ref, mid_ref, ds_far_ref, dq_ref, own_ref = refs[7:14]
    kt_scr, ds_scr, w_scr, near_scr, far_scr = refs[14:]
    rows = q_ref.shape[0]
    pick(across_ref, chip_ref, near_scr, near_scr.shape[1])
    pick(far_ref, across_ref, far_scr, far_scr.shape[1])
    kv_refs = [kv_ref, near_scr, side_ref, far_scr]

    def first(i):
        group = i // PER_GROUP
        if i % PER_GROUP == 0:
            for b, ref in enumerate(kv_refs):
                kt_scr[group, :, at(b, rows)] = ref[:, at(group, HD)].T
        column = at(i, 2 * rows)
        half, part = group % 2, at(i % PER_GROUP, 2 * rows)
        w = p_ref[:, column] * final_ref[1:2, column]
        ds_scr[half, :, part] = (w * (dp_ref[:, column] - final_ref[0:1, column])).astype(BF16)
        w_scr[half, :, part] = w.astype(BF16)

    def second(i):
        half, part = i // PER_GROUP % 2, at(i % PER_GROUP, 2 * rows)
        column = at(i, 2 * rows)
        ds = jnp.concatenate(
            [ds_scr[half, :, part], mid_ref[:, column], ds_far_ref[:, column]], axis=0
        )
        dqt = lax.dot_general(kt_scr[i // PER_GROUP], ds, NN, preferred_element_type=F32)
        dq = (dqt * SCALE).astype(BF16).T
        dq_ref[:, at(2 * i, HD)] = dq[:rows]
        dq_ref[:, at(2 * i + 1, HD)] = dq[rows:]

    def own_grads(group):
        own_ref[:, at(group, HD)] = SCALE * lax.dot_general(
            ds_scr[group % 2], stacked(q_ref, group * GROUP, GROUP), NN, preferred_element_type=F32
        )
        own_ref[:, at(HK + group, HD)] = lax.dot_general(
            w_scr[group % 2], stacked(d_ref, group * GROUP, GROUP), NN, preferred_element_type=F32
        )

    pipelined([first, second, at_group_end(own_grads)])


def call(body, lens, args, outs, scratch, matmul_rows, grant, out_space=pltpu.VMEM):
    specs = [pl.BlockSpec(memory_space=pltpu.SMEM)] * len(lens)
    specs += [pl.BlockSpec(memory_space=pltpu.VMEM)] * len(args)
    docs = sum(x.shape[0] for x in lens)
    return pl.pallas_call(
        functools.partial(body, len(lens)),
        in_specs=specs,
        out_specs=[pl.BlockSpec(memory_space=out_space)] * len(outs),
        out_shape=outs,
        scratch_shapes=([pltpu.SMEM((docs,), jnp.int32)] if lens else []) + scratch,
        cost_estimate=pl.CostEstimate(
            flops=2 * HQ * HD * HD * matmul_rows,
            bytes_accessed=sum(x.size * x.dtype.itemsize for x in list(args) + list(outs)),
            transcendentals=0,
        ),
        compiler_params=pltpu.CompilerParams(vmem_limit_bytes=grant << 20),
    )(*lens, *args)


def on_device(queries, keys_values, out_grads, doc_lengths):
    kv, q, dout = keys_values[0], queries[0], out_grads[0]
    rows, wide = kv.shape
    keys = (REACH + 1) * rows
    array = jax.ShapeDtypeStruct
    block = array((rows, wide), BF16)
    square = array((rows, HQ * rows), F32)
    stat = array((8, HQ * rows), F32)

    def exponentials(even_kv, odd_kv, offset):
        return call(
            functools.partial(block_kernel, offset), (),
            (docs, q, dout, even_kv, odd_kv), [stat, square, square],
            [
                pltpu.VMEM((rows, rows), F32),
                pltpu.VMEM((SLOTS, rows, 2 * rows), F32),
                pltpu.VMEM((rows, wide), BF16),
            ],
            2 * rows, 4,
        )

    across = one_three(kv)
    far = moved(kv, lambda i: i + 3 if i % 2 else -1)
    chip = swapped(kv)
    lens = all_lengths(doc_lengths)
    (causal,) = call(causal_kernel, (), (), [array((rows, rows), F32)], [], 100 * keys, 1)
    s_own, dp_own = call(products_kernel, (), (q, dout, kv), [square, square], [], 2 * rows, 4)
    own_stats, p_own, docs = call(
        own_kernel, lens, (s_own, dp_own, causal),
        [stat, square, array((8, rows), jnp.int32)], [pltpu.VMEM((rows, rows), F32)],
        rows, 2,
    )
    side = swapped(across)
    near_stats, p_near, dp_near = exponentials(across, chip, 1)
    side_stats, p_side, dp_side = exponentials(side, side, 2)
    final, ds_far, g_far = call(
        far_kernel, (),
        (docs, q, dout, far, across, own_stats, near_stats, side_stats),
        [stat, array((rows, HQ * rows), BF16), block],
        [pltpu.VMEM((rows, rows), F32)]
        + [pltpu.VMEM((SLOTS, rows, 2 * rows), F32)] * 3
        + [pltpu.VMEM((SLOTS, 8, 2 * rows), F32)]
        + [pltpu.VMEM((2, rows, GROUP * rows), BF16), pltpu.VMEM((rows, wide), BF16)],
        4 * rows, 6,
    )
    relayed = moved(g_far, lambda i: -1 if i % 2 or i < REACH else i - 2)
    g_near, g_pair, ds_mid = call(
        mid_kernel, (),
        (docs, q, dout, p_near, dp_near, p_side, dp_side, final),
        [
            block,
            array((2 * rows, wide), BF16),
            array((2 * rows, HQ * rows), BF16),
        ],
        [pltpu.VMEM((2, 2 * rows, GROUP * rows), BF16)], 4 * rows, 4,
    )
    pair_back = swapped(g_pair)
    (odd_sum,) = call(odd_sum_kernel, (), (g_far, pair_back), [block], [], 1, 1)
    odd_back = moved(odd_sum, lambda i: i - 3 if i % 2 else -1)
    (joined,) = call(even_sum_kernel, (), (g_near, pair_back, relayed), [block], [], 1, 1)
    even_back = moved(joined, lambda i: -1 if i % 2 else i - 1)
    dq, own = call(
        query_kernel, (),
        (q, dout, kv, across, chip, side, far, p_own, dp_own, final, ds_mid, ds_far),
        [array(q.shape, BF16), array((rows, wide), F32)],
        [pltpu.VMEM((HK, HD, keys), BF16)]
        + [pltpu.VMEM((2, rows, GROUP * rows), BF16)] * 2
        + [pltpu.VMEM((rows, HK * HD), BF16)] * 2,
        2 * rows + keys, 6,
    )
    (total,) = call(
        finish_kernel, (), (own, pair_back, odd_back, even_back), [block],
        [pltpu.VMEM((rows, wide), BF16), pltpu.SemaphoreType.DMA((4,))], 1, 3, pltpu.HBM,
    )
    return (dq[None], total[None])


def solution(mesh):
    spec = P("pipe", "ctx", None)
    return jax.shard_map(
        on_device,
        mesh=mesh,
        in_specs=(spec, spec, spec, P("pipe")),
        out_specs=(spec, spec),
        check_vma=False,
    )
```
